32 devices in a mesh: chan: 8 (over z, x), section: 4 (over y, core).
Axes of the slice: x: 2, y: 2, z: 4, core: 2. Of those that a mesh axis runs over, the one named last changes fastest.
Arguments:
- voltages: bfloat16 [2, 2, 36, 16, 188, 128], P(None, None, 'section', 'chan'), may hold values from -32 to 32
- weights: bfloat16 [2, 36, 16, 36, 188], P(None, 'section', 'chan'), may hold values from -4 to 4
- sat_index: int32 [2, 8, 2], P(None, 'chan'), may hold values from 0 to 63, as said below
- offsets: int32 [2, 128], replicated, may hold values from 0 to 127
- angles: float32 [64, 188], replicated, may hold values from -3 to 3
Outputs:
- visibilities: float32 [2, 36, 16, 1296], P(None, 'section', 'chan')
- new_weights: bfloat16 [2, 36, 16, 36, 188], P(None, 'section', 'chan')
The draws below stay inside these ranges and needn't reach their ends.
Inputs may be any that keep to these rules, and one draw needn't show every extreme that they name: `sat_index`: catalogue rows of the satellites nulled in each cycle and block of 2 channels.
All inputs are finite; a program needn't handle non-finite values.
Results may differ from the reference program's by a relative error of at most 0.0065.
Values may be sent and summed in bfloat16 or wider, within the bound.
No kernel may reach another device: no remote copies, remote signals or barrier semaphores. Data moves between devices by JAX's collectives and lax.ppermute only.
A program may use at most 128 MiB of HBM per device.

```python
import math
import jax
import jax.numpy as jnp
from jax import lax

DISHES = 36
PORTS = 188
BEAMS = 36
TIME = 128
TS = 128
CYCLES = 2
NSAT = 2
K_DIR = 64
BLOCK_CH = 2
CHANNELS = 16
BLOCKS = 8


def catalogue(key):
    phases = jax.random.uniform(jax.random.fold_in(key, 11), (K_DIR, PORTS), jnp.float32, -3.0, 3.0)
    listed = jax.random.randint(jax.random.fold_in(key, 12), (CYCLES, BLOCKS, NSAT), 0, K_DIR, dtype=jnp.int32)
    return (phases, listed)


def draw_angles(key, part):
    return catalogue(key)[0]


def draw_sat_index(key, part):
    return catalogue(key)[1]


def draw_weights(key, part):
    phases, listed = catalogue(key)
    per_channel = jnp.repeat(listed, BLOCK_CH, axis=1)
    present = jnp.moveaxis(per_channel, 0, 1).reshape(CHANNELS, CYCLES * NSAT)
    cosine = jnp.cos(phases)[present]
    sine_part = jnp.sin(phases)[present]
    coeff_shape = (2, DISHES, CHANNELS, BEAMS, CYCLES * NSAT)
    noise_shape = (2, DISHES, CHANNELS, BEAMS, PORTS)
    spread = 0.5 / math.sqrt(PORTS)
    base = 1.0 / math.sqrt(2 * PORTS)
    coeff = jax.random.truncated_normal(jax.random.fold_in(key, 31), -4.0, 4.0, coeff_shape, jnp.float32) * spread
    noise_part = jax.random.truncated_normal(jax.random.fold_in(key, 32), -4.0, 4.0, noise_shape, jnp.float32) * base
    real_part = jnp.einsum('dfbk,fkp->dfbp', coeff[0], cosine) - jnp.einsum('dfbk,fkp->dfbp', coeff[1], sine_part)
    imag_part = jnp.einsum('dfbk,fkp->dfbp', coeff[0], sine_part) + jnp.einsum('dfbk,fkp->dfbp', coeff[1], cosine)
    return (noise_part + jnp.stack([real_part, imag_part])).astype(jnp.bfloat16)


def draw_voltages(key, part):
    phases, listed = catalogue(key)
    per_channel = jnp.repeat(listed, BLOCK_CH, axis=1)
    earlier = jnp.concatenate([per_channel[:1], per_channel[:-1]], axis=0)
    present = jnp.concatenate([per_channel, earlier], axis=2)
    cosine = jnp.cos(phases)[present]
    sine_part = jnp.sin(phases)[present]
    later = jnp.broadcast_to((jnp.arange(CYCLES) > 0).astype(jnp.float32)[:, None], (CYCLES, NSAT))
    active = jnp.concatenate([jnp.ones((CYCLES, NSAT), jnp.float32), later], axis=1)[:, None, :]
    full_shape = (CYCLES, 2, DISHES, CHANNELS, PORTS, TIME)
    noise_part = jax.random.truncated_normal(jax.random.fold_in(key, 21), -4.0, 4.0, full_shape, jnp.float32)
    strength = jnp.exp(jax.random.uniform(jax.random.fold_in(key, 22), (CYCLES, CHANNELS, 2 * NSAT), jnp.float32, math.log(0.03), math.log(0.12)))
    strength = strength * active
    signal = jax.random.truncated_normal(jax.random.fold_in(key, 23), -4.0, 4.0, (CYCLES, 2, DISHES, CHANNELS, 2 * NSAT, TIME), jnp.float32)
    gain_real = strength[..., None] * cosine
    gain_imag = strength[..., None] * sine_part
    real_part = jnp.einsum('cfsp,cdfst->cdfpt', gain_real, signal[:, 0]) - jnp.einsum('cfsp,cdfst->cdfpt', gain_imag, signal[:, 1])
    imag_part = jnp.einsum('cfsp,cdfst->cdfpt', gain_real, signal[:, 1]) + jnp.einsum('cfsp,cdfst->cdfpt', gain_imag, signal[:, 0])
    return (noise_part + jnp.stack([real_part, imag_part], axis=1)).astype(jnp.bfloat16)


def with_ends(array, own_key, low, high):
    longest = array.shape.index(max(array.shape))
    spots = []
    for shift in (0, 1):
        where = [jax.random.randint(jax.random.fold_in(own_key, axis), (), 0, length) for axis, length in enumerate(array.shape)]
        where[longest] = (where[longest] + shift) % array.shape[longest]
        spots.append(tuple(where))
    return array.at[spots[0]].set(low).at[spots[1]].set(high)


def setup_inputs(seed: int = 0) -> dict:
    key_of = jax.random.split(jax.random.key(seed), 6)
    return {
        "voltages": draw_voltages(jax.random.fold_in(key_of[5], 71), 0),
        "weights": draw_weights(jax.random.fold_in(key_of[5], 71), 0),
        "sat_index": draw_sat_index(jax.random.fold_in(key_of[5], 71), 0),
        "offsets": with_ends(jax.random.randint(key_of[3], (CYCLES, TS), 0, TIME), jax.random.fold_in(key_of[3], 1), 0, TIME - 1).astype(jnp.int32),
        "angles": draw_angles(jax.random.fold_in(key_of[5], 71), 0),
    }


LOADING = 100.0
HIGHEST = lax.Precision.HIGHEST


def complex_sums(left_side, right_side, pattern):
    left_wide = left_side.astype(jnp.float32)
    right_wide = right_side.astype(jnp.float32)
    turned = jnp.stack([left_wide[1], -left_wide[0]])
    real_part = jnp.einsum(pattern, left_wide, right_wide, precision=HIGHEST)
    imag_part = jnp.einsum(pattern, turned, right_wide, precision=HIGHEST)
    return jnp.stack([real_part, imag_part])


def beamform(weight, voltage_now):
    weight_wide = weight.astype(jnp.float32)
    voltage_wide = voltage_now.astype(jnp.float32)
    turned = jnp.stack([-weight_wide[1], weight_wide[0]])
    real_part = jnp.einsum('cdfbp,cdfpt->dfbt', weight_wide, voltage_wide, precision=HIGHEST)
    imag_part = jnp.einsum('cdfbp,cdfpt->dfbt', turned, voltage_wide, precision=HIGHEST)
    return jnp.stack([real_part, imag_part]).astype(jnp.bfloat16)


def null_update(weight, smooth, steer_real, steer_imag):
    real_weight = weight[0].astype(jnp.float32)
    imag_weight = weight[1].astype(jnp.float32)
    for slot_index in range(steer_real.shape[1]):
        along_real = steer_real[:, slot_index]
        along_imag = steer_imag[:, slot_index]
        null_real = (jnp.einsum('dfpq,fq->dfp', smooth[0], along_real, precision=HIGHEST)
                     - jnp.einsum('dfpq,fq->dfp', smooth[1], along_imag, precision=HIGHEST)
                     + LOADING * along_real)
        null_imag = (jnp.einsum('dfpq,fq->dfp', smooth[0], along_imag, precision=HIGHEST)
                     + jnp.einsum('dfpq,fq->dfp', smooth[1], along_real, precision=HIGHEST)
                     + LOADING * along_imag)
        inverse = 1.0 / jnp.sum(null_real * null_real + null_imag * null_imag, axis=-1)
        coeff_real = (jnp.einsum('dfp,dfbp->dfb', null_real, real_weight, precision=HIGHEST)
                      + jnp.einsum('dfp,dfbp->dfb', null_imag, imag_weight, precision=HIGHEST)) * inverse[..., None]
        coeff_imag = (jnp.einsum('dfp,dfbp->dfb', null_real, imag_weight, precision=HIGHEST)
                      - jnp.einsum('dfp,dfbp->dfb', null_imag, real_weight, precision=HIGHEST)) * inverse[..., None]
        wide_real = null_real[:, :, None, :]
        wide_imag = null_imag[:, :, None, :]
        real_weight = real_weight - (wide_real * coeff_real[..., None] - wide_imag * coeff_imag[..., None])
        imag_weight = imag_weight - (wide_real * coeff_imag[..., None] + wide_imag * coeff_real[..., None])
    return jnp.stack([real_weight, imag_weight]).astype(jnp.bfloat16)


def correlate(beam_out):
    def single_beam(beam_piece):
        return complex_sums(beam_piece, beam_piece, 'cdft,ceft->fde')

    result_sums = lax.map(single_beam, jnp.moveaxis(beam_out, 3, 0))
    return jnp.moveaxis(result_sums, 0, 1)


def reference(voltages, weights, sat_index, offsets, angles):
    cosine_table = jnp.cos(angles)
    sine_table = jnp.sin(angles)
    current = weights
    visibility = jnp.zeros((2, BEAMS, CHANNELS, DISHES, DISHES), jnp.float32)
    for cycle_index in range(CYCLES):
        listed = jnp.repeat(sat_index[cycle_index], BLOCK_CH, axis=0)
        steer_real = cosine_table[listed]
        steer_imag = sine_table[listed]
        pick_times = offsets[cycle_index]

        def each_dish(dish_items):
            voltage_one = dish_items[0][:, None]
            weight_one = dish_items[1][:, None]
            beam_out = beamform(weight_one, voltage_one)
            sampled = jnp.take(voltage_one, pick_times, axis=4)
            covariance = complex_sums(sampled, sampled, 'cdfpt,cdfqt->dfpq')
            padded = jnp.pad(covariance, ((0, 0), (0, 0), (1, 1), (0, 0), (0, 0)))
            smooth = padded[:, :, :-2] + padded[:, :, 1:-1] + padded[:, :, 2:]
            next_weights = null_update(weight_one, smooth, steer_real, steer_imag)
            return beam_out[:, 0], next_weights[:, 0]

        beam_out, next_weights = lax.map(
            each_dish, (jnp.moveaxis(voltages[cycle_index], 1, 0), jnp.moveaxis(current, 1, 0)))
        beam_out = jnp.moveaxis(beam_out, 0, 1)
        current = jnp.moveaxis(next_weights, 0, 1)
        visibility = visibility + correlate(beam_out)
    visibility = visibility * (1.0 / (CYCLES * TIME))
    return visibility.reshape(2, BEAMS, CHANNELS, DISHES * DISHES), current
```

```python
import functools

import jax
import jax.numpy as jnp
from jax import lax
from jax.experimental import pallas as pl
from jax.experimental.pallas import tpu as pltpu
from jax.sharding import PartitionSpec as P

LOADING = 100.0
F32 = jnp.float32
BF16 = jnp.bfloat16
SUB = 8


def rounded_up(size):
    return -(-size // SUB) * SUB


def spread_matrix(ports, chans):
    port = lax.broadcasted_iota(jnp.int32, (ports, ports * chans), 0) * chans
    lane = lax.broadcasted_iota(jnp.int32, (ports, ports * chans), 1)
    return jnp.where((lane >= port) & (lane < port + chans), 1.0, 0.0).astype(BF16)


def own_channel(rows, rows_per_chan, ports, chans):
    row = lax.broadcasted_iota(jnp.int32, (rows, ports * chans), 0)
    lane = lax.broadcasted_iota(jnp.int32, (rows, ports * chans), 1)
    return lax.rem(lax.div(row, rows_per_chan), chans) == lax.rem(lane, chans)


def split(value):
    high = value.astype(BF16)
    low = (value - high.astype(F32)).astype(BF16)
    return high, low


def dot(left, right):
    return jnp.dot(left, right, preferred_element_type=F32)


def dot_t(left, right):
    return lax.dot_general(left, right, (((1,), (1,)), ((), ())), preferred_element_type=F32)


def beams_of(weight_rows, spread, keep, x_real, x_imag):
    wide = jnp.where(keep, dot(weight_rows, spread), 0.0)
    half = wide.shape[0] // 2
    real, imag = wide[:half], wide[half:]
    on_real = jnp.concatenate([real, -imag]).astype(BF16)
    on_imag = jnp.concatenate([imag, real]).astype(BF16)
    return dot(on_real, x_real) + dot(on_imag, x_imag)


def put_beams(beam_rows, stage, dish, dims):
    groups, chans, group_beams, dishes, pad_beams = dims
    block = 2 * dishes
    for part in range(2):
        for f in range(chans):
            for g in range(groups):
                source = (part * chans + f) * pad_beams + g * group_beams
                first = g * stage_rows(dims) + f * group_beams * block + part * dishes + dish
                stage[pl.ds(first, group_beams, stride=block), :] = beam_rows[
                    source : source + group_beams
                ]


def stage_rows(dims):
    groups, chans, group_beams, dishes, pad_beams = dims
    return rounded_up(chans * group_beams * 2 * dishes)


def flush_beams(stage, out, dims):
    groups = dims[0]
    rows = out.shape[1]
    for g in range(groups):
        first = g * stage_rows(dims)
        out[g] = stage[first : first + rows, :].astype(BF16)


def first_beams_kernel(dims, x_ref, w_ref, out_ref, stage):
    dishes = x_ref.shape[2]
    chans = dims[1]
    ports = w_ref.shape[-1]
    spread = spread_matrix(ports, chans)
    keep = own_channel(w_ref.shape[1], dims[4], ports, chans)
    for d in range(dishes):
        rows = beams_of(w_ref[d], spread, keep, x_ref[0, 0, d], x_ref[0, 1, d])
        put_beams(rows, stage, d, dims)
    flush_beams(stage, out_ref, dims)


def nulls_kernel(sat_ref, sat_dn_ref, sat_up_ref, off_ref, ang_ref, x_ref,
                 own_ref, dn_ref, up_ref, phase, folded):
    cycles, _, dishes, wide, samples = x_ref.shape
    ports = ang_ref.shape[-1]
    chans = wide // ports
    slots = sat_ref.shape[-1]
    per_chan = 2 * slots
    rows = chans * per_chan
    spread = spread_matrix(ports, chans)
    lane_t = lax.broadcasted_iota(jnp.int32, (1, samples), 1)
    for c in range(cycles):
        for f in range(chans):
            beside = sat_dn_ref if f == 0 else sat_up_ref
            for s in range(slots):
                base = f * per_chan + s
                phase[pl.ds(c * rows + base, 1), :] = ang_ref[pl.ds(sat_ref[c, s], 1), :]
                phase[pl.ds(c * rows + base + slots, 1), :] = ang_ref[
                    pl.ds(beside[c, s], 1), :
                ]
    angle = phase[...]
    cosine, sine = jnp.cos(angle), jnp.sin(angle)
    keep4 = own_channel(4 * rows, per_chan, ports, chans)
    keep2 = own_channel(2 * rows, per_chan, ports, chans)
    for c in range(cycles):
        def count(j, total):
            return total + jnp.where(lane_t == off_ref[c, j], 1.0, 0.0)

        counts = lax.fori_loop(0, off_ref.shape[1], count, jnp.zeros((1, samples), F32), unroll=8)
        a_real = cosine[c * rows : (c + 1) * rows]
        a_imag = sine[c * rows : (c + 1) * rows]
        real_h, real_l = split(a_real)
        imag_h, imag_l = split(a_imag)
        column = jnp.concatenate(
            [real_h.astype(F32), real_l.astype(F32), imag_h.astype(F32), imag_l.astype(F32)]
        ).astype(BF16)
        wide_rows = jnp.where(keep4, dot(column, spread), 0.0)
        half = 2 * rows
        on_real = wide_rows.astype(BF16)
        on_imag = jnp.concatenate([wide_rows[half:], -wide_rows[:half]]).astype(BF16)
        for d in range(dishes):
            x_real, x_imag = x_ref[c, 0, d], x_ref[c, 1, d]
            inner = dot(on_real, x_real) + dot(on_imag, x_imag)
            inner_real = (inner[0:rows] + inner[rows:half]) * counts
            inner_imag = (inner[half : half + rows] + inner[half + rows :]) * counts
            real_h, real_l = split(inner_real)
            imag_h, imag_l = split(inner_imag)
            pieces = jnp.concatenate(
                [real_h.astype(F32), real_l.astype(F32), imag_h.astype(F32), imag_l.astype(F32)]
            )
            turned = jnp.concatenate([-pieces[half:], pieces[:half]])
            outer = dot_t(pieces.astype(BF16), x_real) + dot_t(turned.astype(BF16), x_imag)
            both = jnp.concatenate(
                [outer[0:rows] + outer[rows:half], outer[half : half + rows] + outer[half + rows :]]
            )
            first = (c * dishes + d) * 2 * rows
            folded[first : first + 2 * rows, :] = jnp.where(keep2, both, 0.0)
    high, low = split(folded[...])
    summed = dot_t(high, spread) + dot_t(low, spread)
    for c in range(cycles):
        for d in range(dishes):
            first = (c * dishes + d) * 2 * rows
            for part in range(2):
                block = summed[first + part * rows : first + (part + 1) * rows]
                own = block[0:slots]
                for f in range(1, chans):
                    own = own + block[f * per_chan : f * per_chan + slots]
                along = (cosine if part == 0 else sine)[c * rows : c * rows + slots]
                last = (chans - 1) * per_chan + slots
                where = slice(part * slots, (part + 1) * slots)
                own_ref[c, d, where, :] = own + LOADING * along
                dn_ref[c, d, where, :] = block[slots : 2 * slots]
                up_ref[c, d, where, :] = block[last : last + slots]


def null_rows(rows, own, beside, chans, pad_beams):
    slots = own.shape[0] // 2
    half = rows.shape[0] // 2
    reals, imags = [], []
    for f in range(chans):
        real = rows[f * pad_beams : (f + 1) * pad_beams]
        imag = rows[half + f * pad_beams : half + (f + 1) * pad_beams]
        null = own + beside[f]
        for s in range(slots):
            u_real = null[s : s + 1]
            u_imag = null[slots + s : slots + s + 1]
            inverse = 1.0 / jnp.sum(u_real * u_real + u_imag * u_imag, axis=-1, keepdims=True)
            c_real = jnp.sum(real * u_real + imag * u_imag, axis=-1, keepdims=True) * inverse
            c_imag = jnp.sum(imag * u_real - real * u_imag, axis=-1, keepdims=True) * inverse
            real = real - (u_real * c_real - u_imag * c_imag)
            imag = imag - (u_real * c_imag + u_imag * c_real)
        reals.append(real)
        imags.append(imag)
    return jnp.concatenate(reals + imags)


def next_beams_kernel(dims, x_ref, w_ref, own_ref, dn_ref, up_ref, out_ref, next_ref, stage):
    dishes = x_ref.shape[2]
    chans, pad_beams = dims[1], dims[4]
    ports = w_ref.shape[-1]
    spread = spread_matrix(ports, chans)
    keep = own_channel(w_ref.shape[1], pad_beams, ports, chans)
    for d in range(dishes):
        rows = null_rows(
            w_ref[d].astype(F32), own_ref[0, d], (dn_ref[0, d], up_ref[0, d]), chans, pad_beams
        ).astype(BF16)
        next_ref[d] = rows
        put_beams(
            beams_of(rows, spread, keep, x_ref[0, 0, d], x_ref[0, 1, d]), stage, d, dims
        )
    flush_beams(stage, out_ref, dims)


def last_nulls_kernel(dims, w_ref, own_ref, dn_ref, up_ref, next_ref):
    chans, pad_beams = dims[1], dims[4]
    for d in range(w_ref.shape[0]):
        next_ref[d] = null_rows(
            w_ref[d].astype(F32), own_ref[0, d], (dn_ref[0, d], up_ref[0, d]), chans, pad_beams
        ).astype(BF16)


def correlate_kernel(dims, scale, *refs):
    groups, chans, group_beams, dishes, _ = dims
    beam_refs, out_ref, gathered, sums = refs[:-3], refs[-3], refs[-2], refs[-1]
    all_dishes = groups * dishes
    pad_dishes = rounded_up(all_dishes)
    pairs = group_beams * chans
    pad_pairs = rounded_up(pairs)
    samples = gathered.shape[-1]
    block = 2 * dishes
    filler = jnp.zeros((pad_dishes, samples), F32)
    for i in range(len(beam_refs) * pairs * 2):
        gathered[i] = filler
    for i, beam_ref in enumerate(beam_refs):
        for g in range(groups):
            values = beam_ref[g].astype(F32)
            for f in range(chans):
                for b in range(group_beams):
                    for part in range(2):
                        first = (f * group_beams + b) * block + part * dishes
                        gathered[
                            (i * pairs + b * chans + f) * 2 + part,
                            g * dishes : (g + 1) * dishes,
                            :,
                        ] = values[first : first + dishes]
    for pair in range(pairs):
        total = None
        for i in range(len(beam_refs)):
            real = gathered[(i * pairs + pair) * 2]
            imag = gathered[(i * pairs + pair) * 2 + 1]
            top = jnp.concatenate([real, imag], axis=1)
            left = jnp.concatenate([top, jnp.concatenate([imag, -real], axis=1)]).astype(BF16)
            right = jnp.concatenate(
                [top, jnp.zeros((samples - pad_dishes, 2 * samples), F32)]
            ).astype(BF16)
            term = dot_t(left, right)
            total = term if total is None else total + term
        sums[pl.ds(pair, 2 * pad_dishes, stride=pad_pairs), :] = total * scale
    for part in range(2):
        pieces = []
        for d in range(all_dishes):
            first = (part * pad_dishes + d) * pad_pairs
            pieces.append(sums[first : first + pad_pairs, 0:all_dishes])
        flat = jnp.concatenate(pieces, axis=1)
        out_ref[part] = flat[:pairs]


def vmem():
    return pl.BlockSpec(memory_space=pltpu.VMEM)


def smem():
    return pl.BlockSpec(memory_space=pltpu.SMEM)


def per_device(voltages, weights, sat_index, offsets, angles):
    cycles, _, dishes, chans, ports, samples = voltages.shape
    beams = weights.shape[3]
    slots = sat_index.shape[2]
    groups = lax.axis_size("section")
    peers = lax.axis_size("chan")
    group_beams = beams // groups
    pad_beams = rounded_up(beams)
    dims = (groups, chans, group_beams, dishes, pad_beams)
    wide = ports * chans
    x = voltages.transpose(0, 1, 2, 4, 3, 5).reshape(cycles, 2, dishes, wide, samples)
    w = jnp.pad(weights, ((0, 0), (0, 0), (0, 0), (0, pad_beams - beams), (0, 0)))
    w = w.transpose(1, 0, 2, 3, 4).reshape(dishes, 2 * chans * pad_beams, ports)

    up = [(i, i + 1) for i in range(peers - 1)]
    down = [(i + 1, i) for i in range(peers - 1)]
    sat_dn = lax.ppermute(sat_index, "chan", up)
    sat_up = lax.ppermute(sat_index, "chan", down)

    chunk = 2 * chans * group_beams * dishes
    sent = jax.ShapeDtypeStruct((groups, chunk, samples), BF16)
    stage = pltpu.VMEM((groups * stage_rows(dims), samples), F32)
    w_rows = w.shape[1]

    def x_of(cycle):
        return pl.BlockSpec((1, 2, dishes, wide, samples), lambda i: (cycle, 0, 0, 0, 0))

    def whole(*shape):
        return pl.BlockSpec(shape, lambda i: (0,) * len(shape))

    first = pl.pallas_call(
        functools.partial(first_beams_kernel, dims),
        grid=(1,),
        out_shape=sent,
        in_specs=[x_of(0), whole(*w.shape)],
        out_specs=whole(*sent.shape),
        scratch_shapes=[stage],
        name="first_beams",
    )(x, w)
    first_all = lax.all_to_all(first, "section", split_axis=0, concat_axis=0, tiled=True)

    rows = chans * 2 * slots
    vectors = jax.ShapeDtypeStruct((cycles, dishes, 2 * slots, ports), F32)
    own, to_dn, to_up = pl.pallas_call(
        nulls_kernel,
        out_shape=(vectors,) * 3,
        in_specs=[smem(), smem(), smem(), smem(), vmem(), vmem()],
        out_specs=(vmem(),) * 3,
        scratch_shapes=[
            pltpu.VMEM((cycles * rows, ports), F32),
            pltpu.VMEM((cycles * dishes * 2 * rows, wide), F32),
        ],
        name="nulls",
    )(sat_index[:, 0], sat_dn[:, 0], sat_up[:, 0], offsets, angles, x)
    from_up = lax.ppermute(to_dn, "chan", down)
    from_dn = lax.ppermute(to_up, "chan", up)

    def vec_of(cycle):
        return pl.BlockSpec((1, dishes, 2 * slots, ports), lambda i: (cycle, 0, 0, 0))

    second, w_next = pl.pallas_call(
        functools.partial(next_beams_kernel, dims),
        grid=(1,),
        out_shape=(sent, jax.ShapeDtypeStruct(w.shape, BF16)),
        in_specs=[x_of(1), whole(*w.shape), vec_of(0), vec_of(0), vec_of(0)],
        out_specs=(whole(*sent.shape), whole(*w.shape)),
        scratch_shapes=[stage],
        name="next_beams",
    )(x, w, own, from_dn, from_up)
    second_all = lax.all_to_all(second, "section", split_axis=0, concat_axis=0, tiled=True)

    w_last = pl.pallas_call(
        functools.partial(last_nulls_kernel, dims),
        grid=(1,),
        out_shape=jax.ShapeDtypeStruct(w.shape, BF16),
        in_specs=[whole(*w.shape), vec_of(1), vec_of(1), vec_of(1)],
        out_specs=whole(*w.shape),
        name="last_nulls",
    )(w_next, own, from_dn, from_up)
    new_weights = w_last.reshape(dishes, 2, chans, pad_beams, ports)[:, :, :, :beams]
    new_weights = new_weights.transpose(1, 0, 2, 3, 4)

    all_dishes = dishes * groups
    pairs = group_beams * chans
    pad_dishes = rounded_up(all_dishes)
    vis = pl.pallas_call(
        functools.partial(correlate_kernel, dims, 1.0 / (cycles * samples)),
        out_shape=jax.ShapeDtypeStruct((2, pairs, all_dishes * all_dishes), F32),
        in_specs=[vmem(), vmem()],
        out_specs=vmem(),
        scratch_shapes=[
            pltpu.VMEM((cycles * pairs * 2, pad_dishes, samples), F32),
            pltpu.VMEM((2 * pad_dishes * rounded_up(pairs), samples), F32),
        ],
        name="correlate",
    )(first_all, second_all)
    vis = vis.reshape(2, group_beams, chans, all_dishes * all_dishes)
    return vis, new_weights


def solution(mesh):
    placed = (
        P(None, None, "section", "chan", None, None),
        P(None, "section", "chan", None, None),
        P(None, "chan", None),
        P(),
        P(),
    )
    return jax.shard_map(
        per_device,
        mesh=mesh,
        in_specs=placed,
        out_specs=(P(None, "section", "chan", None), P(None, "section", "chan", None, None)),
        check_vma=False,
    )
```

```python
import functools

import jax
import jax.numpy as jnp
from jax import lax
from jax.experimental import pallas as pl
from jax.experimental.pallas import tpu as pltpu
from jax.sharding import PartitionSpec as P


LOADING = 100.0
F32 = jnp.float32
BF16 = jnp.bfloat16
SUB = 8
VMEM_GRANT = 20 * 1024 * 1024


def partner(index, step, count):
    if count & (count - 1) == 0:
        return index ^ step
    return lax.rem(index + step, count)


def source_of(index, step, count):
    if count & (count - 1) == 0:
        return index ^ step
    return lax.rem(index + count - step, count)


def rounded_up(size):
    return -(-size // SUB) * SUB


def spread_matrix(ports, chans):
    port = lax.broadcasted_iota(jnp.int32, (ports, ports * chans), 0) * chans
    lane = lax.broadcasted_iota(jnp.int32, (ports, ports * chans), 1)
    return jnp.where((lane >= port) & (lane < port + chans), 1.0, 0.0).astype(BF16)


def own_channel(rows, rows_per_chan, ports, chans):
    row = lax.broadcasted_iota(jnp.int32, (rows, ports * chans), 0)
    lane = lax.broadcasted_iota(jnp.int32, (rows, ports * chans), 1)
    return lax.rem(lax.div(row, rows_per_chan), chans) == lax.rem(lane, chans)


def split(value):
    high = value.astype(BF16)
    low = (value - high.astype(F32)).astype(BF16)
    return high, low


def dot(left, right):
    return jnp.dot(left, right, preferred_element_type=F32)


def dot_t(left, right):
    return lax.dot_general(left, right, (((1,), (1,)), ((), ())), preferred_element_type=F32)


def beams_of(weight_rows, spread, keep, x_real, x_imag):
    wide = jnp.where(keep, dot(weight_rows, spread), 0.0)
    half = wide.shape[0] // 2
    real, imag = wide[:half], wide[half:]
    on_real = jnp.concatenate([real, -imag]).astype(BF16)
    on_imag = jnp.concatenate([imag, real]).astype(BF16)
    return dot(on_real, x_real) + dot(on_imag, x_imag)


def put_beams(beam_rows, stage, dish, dims):
    groups, chans, group_beams, dishes, pad_beams = dims
    block = 2 * dishes
    for part in range(2):
        for f in range(chans):
            for g in range(groups):
                source = (part * chans + f) * pad_beams + g * group_beams
                first = g * stage_rows(dims) + f * group_beams * block + part * dishes + dish
                stage[pl.ds(first, group_beams, stride=block), :] = beam_rows[
                    source : source + group_beams
                ]


def stage_rows(dims):
    _, chans, group_beams, dishes, _ = dims
    return rounded_up(chans * group_beams * 2 * dishes)


def flush_beams(stage, outs, dims):
    me = lax.axis_index("section")
    rows = outs[0].shape[0]
    for k, out in enumerate(outs):
        first = pl.multiple_of(partner(me, k, dims[0]) * stage_rows(dims), SUB)
        out[...] = stage[pl.ds(first, stage_rows(dims)), :][:rows].astype(BF16)


def weight_rows_of(w_ref, d, pad_beams):
    parts, _, chans, beams, ports = w_ref.shape
    pieces = []
    for part in range(parts):
        for f in range(chans):
            pieces.append(w_ref[part, d, f].astype(F32))
            if pad_beams > beams:
                pieces.append(jnp.zeros((pad_beams - beams, ports), F32))
    return jnp.concatenate(pieces)


def first_beams_kernel(dims, x_ref, w_ref, *refs):
    outs, stage = refs[:-1], refs[-1]
    dishes = x_ref.shape[2]
    chans, pad_beams = dims[1], dims[4]
    ports = w_ref.shape[-1]
    spread = spread_matrix(ports, chans)
    keep = own_channel(2 * chans * pad_beams, pad_beams, ports, chans)
    for d in range(dishes):
        rows = weight_rows_of(w_ref, d, pad_beams).astype(BF16)
        put_beams(beams_of(rows, spread, keep, x_ref[0, 0, d], x_ref[0, 1, d]), stage, d, dims)
    flush_beams(stage, outs, dims)


def even_place():
    return lax.rem(lax.axis_index("chan"), 2) == 0


def nulls_kernel(sat_ref, sat_a_ref, sat_b_ref, off_ref, ang_ref, x_ref,
                 own_ref, a_ref, b_ref, phase, folded):
    cycles, _, dishes, wide, samples = x_ref.shape
    ports = ang_ref.shape[-1]
    chans = wide // ports
    slots = sat_ref.shape[-1]
    per_chan = 2 * slots
    rows = chans * per_chan
    spread = spread_matrix(ports, chans)
    even = even_place()
    place = lax.axis_index("chan")
    last_place = lax.axis_size("chan") - 1
    time = lax.broadcasted_iota(jnp.int32, (samples, off_ref.shape[1]), 0)
    ones = jnp.ones((rows, off_ref.shape[1]), BF16)
    for c in range(cycles):
        for f in range(chans):
            swapped = even if f == 0 else jnp.logical_not(even)
            for s in range(slots):
                base = f * per_chan + s
                phase[pl.ds(c * rows + base, 1), :] = ang_ref[pl.ds(sat_ref[c, s], 1), :]
                phase[pl.ds(c * rows + base + slots, 1), :] = ang_ref[
                    pl.ds(jnp.where(swapped, sat_b_ref[c, s], sat_a_ref[c, s]), 1), :
                ]
    angle = phase[...]
    cosine, sine = jnp.cos(angle), jnp.sin(angle)
    keep4 = own_channel(4 * rows, per_chan, ports, chans)
    keep2 = own_channel(2 * rows, per_chan, ports, chans)
    for c in range(cycles):
        hits = jnp.where(time == off_ref[c : c + 1, :], 1.0, 0.0).astype(BF16)
        counts = dot_t(ones, hits)
        a_real = cosine[c * rows : (c + 1) * rows]
        a_imag = sine[c * rows : (c + 1) * rows]
        real_h, real_l = split(a_real)
        imag_h, imag_l = split(a_imag)
        column = jnp.concatenate(
            [real_h.astype(F32), real_l.astype(F32), imag_h.astype(F32), imag_l.astype(F32)]
        ).astype(BF16)
        wide_rows = jnp.where(keep4, dot(column, spread), 0.0)
        half = 2 * rows
        on_real = wide_rows.astype(BF16)
        on_imag = jnp.concatenate([wide_rows[half:], -wide_rows[:half]]).astype(BF16)
        for d in range(dishes):
            x_real, x_imag = x_ref[c, 0, d], x_ref[c, 1, d]
            inner = dot(on_real, x_real) + dot(on_imag, x_imag)
            inner_real = (inner[0:rows] + inner[rows:half]) * counts
            inner_imag = (inner[half : half + rows] + inner[half + rows :]) * counts
            real_h, real_l = split(inner_real)
            imag_h, imag_l = split(inner_imag)
            pieces = jnp.concatenate(
                [real_h.astype(F32), real_l.astype(F32), imag_h.astype(F32), imag_l.astype(F32)]
            )
            turned = jnp.concatenate([-pieces[half:], pieces[:half]])
            outer = dot_t(pieces.astype(BF16), x_real) + dot_t(turned.astype(BF16), x_imag)
            both = jnp.concatenate(
                [outer[0:rows] + outer[rows:half], outer[half : half + rows] + outer[half + rows :]]
            )
            first = (c * dishes + d) * 2 * rows
            folded[first : first + 2 * rows, :] = jnp.where(keep2, both, 0.0)
    high, low = split(folded[...])
    summed = dot_t(high, spread) + dot_t(low, spread)
    for c in range(cycles):
        for d in range(dishes):
            first = (c * dishes + d) * 2 * rows
            for part in range(2):
                block = summed[first + part * rows : first + (part + 1) * rows]
                own = block[0:slots]
                for f in range(1, chans):
                    own = own + block[f * per_chan : f * per_chan + slots]
                along = (cosine if part == 0 else sine)[c * rows : c * rows + slots]
                last = (chans - 1) * per_chan + slots
                where = slice(part * slots, (part + 1) * slots)
                own_ref[c, d, where, :] = own + LOADING * along
                to_dn = jnp.where(place > 0, block[slots : 2 * slots], 0.0)
                to_up = jnp.where(place < last_place, block[last : last + slots], 0.0)
                a_ref[c, d, where, :] = jnp.where(even, to_up, to_dn)
                b_ref[c, d, where, :] = jnp.where(even, to_dn, to_up)


def null_rows(rows, own, beside, chans, pad_beams):
    slots = own.shape[0] // 2
    half = rows.shape[0] // 2
    reals, imags = [], []
    for f in range(chans):
        real = rows[f * pad_beams : (f + 1) * pad_beams]
        imag = rows[half + f * pad_beams : half + (f + 1) * pad_beams]
        null = own + beside[f]
        for s in range(slots):
            u_real = null[s : s + 1]
            u_imag = null[slots + s : slots + s + 1]
            inverse = 1.0 / jnp.sum(u_real * u_real + u_imag * u_imag, axis=-1, keepdims=True)
            c_real = jnp.sum(real * u_real + imag * u_imag, axis=-1, keepdims=True) * inverse
            c_imag = jnp.sum(imag * u_real - real * u_imag, axis=-1, keepdims=True) * inverse
            real = real - (u_real * c_real - u_imag * c_imag)
            imag = imag - (u_real * c_imag + u_imag * c_real)
        reals.append(real)
        imags.append(imag)
    return jnp.concatenate(reals + imags)


def beside_of(a_ref, b_ref, cycle, d):
    even = even_place()
    a, b = a_ref[cycle, d], b_ref[cycle, d]
    return jnp.where(even, b, a), jnp.where(even, a, b)


def next_beams_kernel(dims, cycle, x_ref, w_ref, own_ref, a_ref, b_ref, *refs):
    outs, next_ref, stage = refs[:-2], refs[-2], refs[-1]
    dishes = x_ref.shape[2]
    chans, pad_beams = dims[1], dims[4]
    ports = w_ref.shape[-1]
    spread = spread_matrix(ports, chans)
    keep = own_channel(2 * chans * pad_beams, pad_beams, ports, chans)
    for d in range(dishes):
        rows = null_rows(
            weight_rows_of(w_ref, d, pad_beams),
            own_ref[cycle, d],
            beside_of(a_ref, b_ref, cycle, d),
            chans,
            pad_beams,
        ).astype(BF16)
        next_ref[d] = rows
        put_beams(
            beams_of(rows, spread, keep, x_ref[cycle + 1, 0, d], x_ref[cycle + 1, 1, d]),
            stage,
            d,
            dims,
        )
    flush_beams(stage, outs, dims)


def last_nulls_kernel(dims, cycle, w_ref, own_ref, a_ref, b_ref, out_ref):
    chans, pad_beams = dims[1], dims[4]
    beams = out_ref.shape[3]
    for d in range(w_ref.shape[0]):
        rows = null_rows(
            w_ref[d].astype(F32),
            own_ref[cycle, d],
            beside_of(a_ref, b_ref, cycle, d),
            chans,
            pad_beams,
        )
        for part in range(2):
            for f in range(chans):
                first = (part * chans + f) * pad_beams
                out_ref[part, d, f] = rows[first : first + beams].astype(BF16)


def correlate_kernel(dims, scale, *refs):
    groups, chans, group_beams, dishes, _ = dims
    beam_refs, out_ref, gathered, sums = refs[:-3], refs[-3], refs[-2], refs[-1]
    all_dishes = groups * dishes
    pad_dishes = rounded_up(all_dishes)
    pairs = group_beams * chans
    pad_pairs = rounded_up(pairs)
    samples = gathered.shape[-1]
    block = 2 * dishes
    filler = jnp.zeros((pad_dishes, samples), F32)
    for i in range(len(beam_refs) // groups * pairs * 2):
        gathered[i] = filler
    me = lax.axis_index("section")
    cycles = len(beam_refs) // groups
    for i in range(cycles):
        for k in range(groups):
            values = beam_refs[i * groups + k][...].astype(F32)
            start = source_of(me, k, groups) * dishes
            for f in range(chans):
                for b in range(group_beams):
                    for part in range(2):
                        first = (f * group_beams + b) * block + part * dishes
                        gathered[
                            (i * pairs + b * chans + f) * 2 + part,
                            pl.ds(start, dishes),
                            :,
                        ] = values[first : first + dishes]
    for pair in range(pairs):
        total = None
        for i in range(cycles):
            real = gathered[(i * pairs + pair) * 2]
            imag = gathered[(i * pairs + pair) * 2 + 1]
            top = jnp.concatenate([real, imag], axis=1)
            left = jnp.concatenate([top, jnp.concatenate([imag, -real], axis=1)]).astype(BF16)
            right = jnp.concatenate(
                [top, jnp.zeros((samples - pad_dishes, 2 * samples), F32)]
            ).astype(BF16)
            term = dot_t(left, right)
            total = term if total is None else total + term
        sums[pl.ds(pair, 2 * pad_dishes, stride=pad_pairs), :] = total * scale
    for part in range(2):
        pieces = []
        for d in range(all_dishes):
            first = (part * pad_dishes + d) * pad_pairs
            pieces.append(sums[first : first + pad_pairs, 0:all_dishes])
        flat = jnp.concatenate(pieces, axis=1)
        for b in range(group_beams):
            out_ref[part, b] = flat[b * chans : (b + 1) * chans]


def vmem():
    return pl.BlockSpec(memory_space=pltpu.VMEM)


def smem():
    return pl.BlockSpec(memory_space=pltpu.SMEM)


def per_device(voltages, weights, sat_index, offsets, angles):
    cycles, _, dishes, chans, ports, samples = voltages.shape
    beams = weights.shape[3]
    slots = sat_index.shape[2]
    groups = lax.axis_size("section")
    peers = lax.axis_size("chan")
    group_beams = beams // groups
    pad_beams = rounded_up(beams)
    assert cycles == 2 and chans == 2 and sat_index.shape[1] == 1
    dims = (groups, chans, group_beams, dishes, pad_beams)
    wide = ports * chans
    x = voltages.transpose(0, 1, 2, 4, 3, 5).reshape(cycles, 2, dishes, wide, samples)

    def pairs_of(first):
        swaps = []
        for i in range(peers):
            other = i + 1 if i % 2 == first else i - 1
            swaps.append((i, other if 0 <= other < peers else i))
        return swaps

    def params(**more):
        return pltpu.CompilerParams(vmem_limit_bytes=VMEM_GRANT, **more)

    def exchange(chunks):
        got = [chunks[0]]
        for k in range(1, groups):
            path = [(i, int(partner(i, k, groups))) for i in range(groups)]
            got.append(lax.ppermute(chunks[k], "section", path))
        return got

    sat_a = lax.ppermute(sat_index, "chan", pairs_of(0))
    sat_b = lax.ppermute(sat_index, "chan", pairs_of(1))

    chunk = 2 * chans * group_beams * dishes
    sent = (jax.ShapeDtypeStruct((chunk, samples), BF16),) * groups
    stage = pltpu.VMEM((groups * stage_rows(dims), samples), F32)

    first = pl.pallas_call(
        functools.partial(first_beams_kernel, dims),
        out_shape=sent,
        in_specs=[vmem()] * 2,
        out_specs=(vmem(),) * groups,
        scratch_shapes=[stage],
        compiler_params=params(),
        name="first_beams",
    )(x, weights)
    first_all = exchange(first)

    rows = chans * 2 * slots
    vectors = jax.ShapeDtypeStruct((cycles, dishes, 2 * slots, ports), F32)
    own, to_a, to_b = pl.pallas_call(
        nulls_kernel,
        out_shape=(vectors,) * 3,
        in_specs=[smem(), smem(), smem(), vmem(), vmem(), vmem()],
        out_specs=(vmem(),) * 3,
        scratch_shapes=[
            pltpu.VMEM((cycles * rows, ports), F32),
            pltpu.VMEM((cycles * dishes * 2 * rows, wide), F32),
        ],
        compiler_params=params(),
        name="nulls",
    )(sat_index[:, 0], sat_a[:, 0], sat_b[:, 0], offsets, angles, x)
    from_a = lax.ppermute(to_a, "chan", pairs_of(0))
    from_b = lax.ppermute(to_b, "chan", pairs_of(1))

    next_rows = jax.ShapeDtypeStruct((dishes, 2 * chans * pad_beams, ports), BF16)
    *second, w_next = pl.pallas_call(
        functools.partial(next_beams_kernel, dims, 0),
        out_shape=(*sent, next_rows),
        in_specs=[vmem()] * 5,
        out_specs=(vmem(),) * (groups + 1),
        scratch_shapes=[stage],
        compiler_params=params(),
        name="next_beams",
    )(x, weights, own, from_a, from_b)
    second_all = exchange(second)

    new_weights = pl.pallas_call(
        functools.partial(last_nulls_kernel, dims, 1),
        out_shape=jax.ShapeDtypeStruct(weights.shape, BF16),
        in_specs=[vmem()] * 4,
        out_specs=vmem(),
        compiler_params=params(),
        name="last_nulls",
    )(w_next, own, from_a, from_b)

    all_dishes = dishes * groups
    pairs = group_beams * chans
    pad_dishes = rounded_up(all_dishes)
    vis = pl.pallas_call(
        functools.partial(correlate_kernel, dims, 1.0 / (cycles * samples)),
        out_shape=jax.ShapeDtypeStruct((2, group_beams, chans, all_dishes * all_dishes), F32),
        in_specs=[vmem()] * (2 * groups),
        out_specs=vmem(),
        scratch_shapes=[
            pltpu.VMEM((cycles * pairs * 2, pad_dishes, samples), F32),
            pltpu.VMEM((2 * pad_dishes * rounded_up(pairs), samples), F32),
        ],
        compiler_params=params(),
        name="correlate",
    )(*first_all, *second_all)
    return vis, new_weights


def solution(mesh):
    placed = (
        P(None, None, "section", "chan", None, None),
        P(None, "section", "chan", None, None),
        P(None, "chan", None),
        P(),
        P(),
    )
    return jax.shard_map(
        per_device,
        mesh=mesh,
        in_specs=placed,
        out_specs=(P(None, "section", "chan", None), P(None, "section", "chan", None, None)),
        check_vma=False,
    )
```

```python
import functools

import jax
import jax.numpy as jnp
from jax import lax
from jax.experimental import pallas as pl
from jax.experimental.pallas import tpu as pltpu
from jax.sharding import PartitionSpec as P


LOADING = 100.0
F32 = jnp.float32
BF16 = jnp.bfloat16
SUB = 8
VMEM_GRANT = 20 * 1024 * 1024


def rounded_up(size):
    return -(-size // SUB) * SUB


def spread_matrix(ports, chans):
    port = lax.broadcasted_iota(jnp.int32, (ports, ports * chans), 0) * chans
    lane = lax.broadcasted_iota(jnp.int32, (ports, ports * chans), 1)
    return jnp.where((lane >= port) & (lane < port + chans), 1.0, 0.0).astype(BF16)


def own_channel(rows, rows_per_chan, ports, chans):
    row = lax.broadcasted_iota(jnp.int32, (rows, ports * chans), 0)
    lane = lax.broadcasted_iota(jnp.int32, (rows, ports * chans), 1)
    return lax.rem(lax.div(row, rows_per_chan), chans) == lax.rem(lane, chans)


def split(value):
    high = value.astype(BF16)
    low = (value - high.astype(F32)).astype(BF16)
    return high, low


def dot(left, right):
    return jnp.dot(left, right, preferred_element_type=F32)


def dot_t(left, right):
    return lax.dot_general(left, right, (((1,), (1,)), ((), ())), preferred_element_type=F32)


def beams_of(weight_rows, spread, keep, x_real, x_imag):
    wide = jnp.where(keep, dot(weight_rows, spread), 0.0)
    half = wide.shape[0] // 2
    real, imag = wide[:half], wide[half:]
    on_real = jnp.concatenate([real, -imag]).astype(BF16)
    on_imag = jnp.concatenate([imag, real]).astype(BF16)
    return dot(on_real, x_real) + dot(on_imag, x_imag)


def put_beams(beam_rows, stage, dish, dims):
    groups, chans, group_beams, dishes, pad_beams = dims
    block = 2 * dishes
    for part in range(2):
        for f in range(chans):
            for g in range(groups):
                source = (part * chans + f) * pad_beams + g * group_beams
                first = g * stage_rows(dims) + f * group_beams * block + part * dishes + dish
                stage[pl.ds(first, group_beams, stride=block), :] = beam_rows[
                    source : source + group_beams
                ]


def stage_rows(dims):
    _, chans, group_beams, dishes, _ = dims
    return rounded_up(chans * group_beams * 2 * dishes)


def flush_beams(stage, outs, steps, dims):
    me = lax.axis_index("section")
    rows = outs[0].shape[0]
    for k, out in zip(steps, outs):
        first = pl.multiple_of((me ^ k) * stage_rows(dims), SUB)
        out[...] = stage[pl.ds(first, stage_rows(dims)), :][:rows].astype(BF16)


def weight_rows_of(w_ref, d, pad_beams):
    parts, _, chans, beams, ports = w_ref.shape
    pieces = []
    for part in range(parts):
        for f in range(chans):
            pieces.append(w_ref[part, d, f].astype(F32))
            if pad_beams > beams:
                pieces.append(jnp.zeros((pad_beams - beams, ports), F32))
    return jnp.concatenate(pieces)


def first_beams_kernel(dims, x_ref, w_ref, *refs):
    (near, mine, *far), (stage, held, sems) = refs[:-3], refs[-3:]
    dishes = x_ref.shape[2]
    chans, pad_beams = dims[1], dims[4]
    copies = []
    for d in range(dishes):
        copies.append(pltpu.make_async_copy(x_ref.at[0, :, d], held.at[:, d], sems.at[d]))
        copies[d].start()
    ports = w_ref.shape[-1]
    spread = spread_matrix(ports, chans)
    keep = own_channel(2 * chans * pad_beams, pad_beams, ports, chans)
    for d in range(dishes):
        rows = weight_rows_of(w_ref, d, pad_beams).astype(BF16)
        copies[d].wait()
        put_beams(beams_of(rows, spread, keep, held[0, d], held[1, d]), stage, d, dims)
    flush_beams(stage, [mine, near], [0, 1], dims)
    for i, out in enumerate(far):
        flush_beams(stage, [out.at[0], out.at[1]], [2 * i + 2, 2 * i + 3], dims)


def even_place():
    return lax.rem(lax.axis_index("chan"), 2) == 0


def nulls_kernel(sat_ref, sat_a_ref, sat_b_ref, off_ref, ang_ref, x_ref,
                 own_ref, a_ref, b_ref, phase, folded):
    cycles, _, dishes, wide, samples = x_ref.shape
    ports = ang_ref.shape[-1]
    chans = wide // ports
    slots = sat_ref.shape[-1]
    per_chan = 2 * slots
    rows = chans * per_chan
    spread = spread_matrix(ports, chans)
    even = even_place()
    place = lax.axis_index("chan")
    last_place = lax.axis_size("chan") - 1
    time = lax.broadcasted_iota(jnp.int32, (samples, off_ref.shape[1]), 0)
    ones = jnp.ones((rows, off_ref.shape[1]), BF16)
    for c in range(cycles):
        for f in range(chans):
            swapped = even if f == 0 else jnp.logical_not(even)
            for s in range(slots):
                base = f * per_chan + s
                phase[pl.ds(c * rows + base, 1), :] = ang_ref[pl.ds(sat_ref[c, s], 1), :]
                phase[pl.ds(c * rows + base + slots, 1), :] = ang_ref[
                    pl.ds(jnp.where(swapped, sat_b_ref[c, s], sat_a_ref[c, s]), 1), :
                ]
    angle = phase[...]
    cosine, sine = jnp.cos(angle), jnp.sin(angle)
    keep4 = own_channel(4 * rows, per_chan, ports, chans)
    keep2 = own_channel(2 * rows, per_chan, ports, chans)
    for c in range(cycles):
        hits = jnp.where(time == off_ref[c : c + 1, :], 1.0, 0.0).astype(BF16)
        counts = dot_t(ones, hits)
        a_real = cosine[c * rows : (c + 1) * rows]
        a_imag = sine[c * rows : (c + 1) * rows]
        real_h, real_l = split(a_real)
        imag_h, imag_l = split(a_imag)
        column = jnp.concatenate(
            [real_h.astype(F32), real_l.astype(F32), imag_h.astype(F32), imag_l.astype(F32)]
        ).astype(BF16)
        wide_rows = jnp.where(keep4, dot(column, spread), 0.0)
        half = 2 * rows
        on_real = wide_rows.astype(BF16)
        on_imag = jnp.concatenate([wide_rows[half:], -wide_rows[:half]]).astype(BF16)
        for d in range(dishes):
            x_real, x_imag = x_ref[c, 0, d], x_ref[c, 1, d]
            inner = dot(on_real, x_real) + dot(on_imag, x_imag)
            inner_real = (inner[0:rows] + inner[rows:half]) * counts
            inner_imag = (inner[half : half + rows] + inner[half + rows :]) * counts
            real_h, real_l = split(inner_real)
            imag_h, imag_l = split(inner_imag)
            pieces = jnp.concatenate(
                [real_h.astype(F32), real_l.astype(F32), imag_h.astype(F32), imag_l.astype(F32)]
            )
            turned = jnp.concatenate([-pieces[half:], pieces[:half]])
            outer = dot_t(pieces.astype(BF16), x_real) + dot_t(turned.astype(BF16), x_imag)
            both = jnp.concatenate(
                [outer[0:rows] + outer[rows:half], outer[half : half + rows] + outer[half + rows :]]
            )
            first = (c * dishes + d) * 2 * rows
            folded[first : first + 2 * rows, :] = jnp.where(keep2, both, 0.0)
    high, low = split(folded[...])
    summed = dot_t(high, spread) + dot_t(low, spread)
    for c in range(cycles):
        for d in range(dishes):
            first = (c * dishes + d) * 2 * rows
            for part in range(2):
                block = summed[first + part * rows : first + (part + 1) * rows]
                own = block[0:slots]
                for f in range(1, chans):
                    own = own + block[f * per_chan : f * per_chan + slots]
                along = (cosine if part == 0 else sine)[c * rows : c * rows + slots]
                last = (chans - 1) * per_chan + slots
                where = slice(part * slots, (part + 1) * slots)
                own_ref[c, d, where, :] = own + LOADING * along
                to_dn = jnp.where(place > 0, block[slots : 2 * slots], 0.0)
                to_up = jnp.where(place < last_place, block[last : last + slots], 0.0)
                a_ref[c, d, where, :] = jnp.where(even, to_up, to_dn)
                b_ref[c, d, where, :] = jnp.where(even, to_dn, to_up)


def null_rows(rows, own, beside, chans, pad_beams):
    slots = own.shape[0] // 2
    half = rows.shape[0] // 2
    reals, imags = [], []
    for f in range(chans):
        real = rows[f * pad_beams : (f + 1) * pad_beams]
        imag = rows[half + f * pad_beams : half + (f + 1) * pad_beams]
        null = own + beside[f]
        for s in range(slots):
            u_real = null[s : s + 1]
            u_imag = null[slots + s : slots + s + 1]
            inverse = 1.0 / jnp.sum(u_real * u_real + u_imag * u_imag, axis=-1, keepdims=True)
            c_real = jnp.sum(real * u_real + imag * u_imag, axis=-1, keepdims=True) * inverse
            c_imag = jnp.sum(imag * u_real - real * u_imag, axis=-1, keepdims=True) * inverse
            real = real - (u_real * c_real - u_imag * c_imag)
            imag = imag - (u_real * c_imag + u_imag * c_real)
        reals.append(real)
        imags.append(imag)
    return jnp.concatenate(reals + imags)


def beside_of(a_ref, b_ref, cycle, d):
    even = even_place()
    a, b = a_ref[cycle, d], b_ref[cycle, d]
    return jnp.where(even, b, a), jnp.where(even, a, b)


def next_beams_kernel(dims, cycle, x_ref, w_ref, own_ref, a_ref, b_ref, near_ref, *refs):
    groups = dims[0]
    passed, (near, mine, *far), (next_ref, stage) = refs[: groups // 2 - 1], refs[groups // 2 - 1 : -2], refs[-2:]
    near[0] = near_ref[...]
    for i, passed_ref in enumerate(passed):
        near[i + 1] = passed_ref[1]
    dishes = x_ref.shape[2]
    chans, pad_beams = dims[1], dims[4]
    ports = w_ref.shape[-1]
    spread = spread_matrix(ports, chans)
    keep = own_channel(2 * chans * pad_beams, pad_beams, ports, chans)
    for d in range(dishes):
        rows = null_rows(
            weight_rows_of(w_ref, d, pad_beams),
            own_ref[cycle, d],
            beside_of(a_ref, b_ref, cycle, d),
            chans,
            pad_beams,
        ).astype(BF16)
        next_ref[d] = rows
        put_beams(
            beams_of(rows, spread, keep, x_ref[cycle + 1, 0, d], x_ref[cycle + 1, 1, d]),
            stage,
            d,
            dims,
        )
    flush_beams(stage, [mine, near.at[groups // 2], *far], range(groups), dims)


def last_nulls_kernel(dims, cycle, w_ref, own_ref, a_ref, b_ref, out_ref):
    chans, pad_beams = dims[1], dims[4]
    beams = out_ref.shape[3]
    for d in range(w_ref.shape[0]):
        rows = null_rows(
            w_ref[d].astype(F32),
            own_ref[cycle, d],
            beside_of(a_ref, b_ref, cycle, d),
            chans,
            pad_beams,
        )
        for part in range(2):
            for f in range(chans):
                first = (part * chans + f) * pad_beams
                out_ref[part, d, f] = rows[first : first + beams].astype(BF16)


def correlate_kernel(dims, scale, *refs):
    groups, chans, group_beams, dishes, _ = dims
    beam_refs, out_ref, gathered, sums = refs[:-3], refs[-3], refs[-2], refs[-1]
    all_dishes = groups * dishes
    pad_dishes = rounded_up(all_dishes)
    pairs = group_beams * chans
    pad_pairs = rounded_up(pairs)
    samples = gathered.shape[-1]
    block = 2 * dishes
    filler = jnp.zeros((pad_dishes, samples), F32)
    for i in range(gathered.shape[0]):
        gathered[i] = filler
    me = lax.axis_index("section")
    cycles = 2
    mine, near, far = beam_refs[:2], beam_refs[2], beam_refs[3:]
    blocks = [(0, 0, mine[0].at[...]), (1, 0, mine[1].at[...])]
    for i in range(groups // 2):
        blocks.append((0, 2 * i + 1, near.at[i]))
    blocks.append((1, 1, near.at[groups // 2]))
    for i in range(groups // 2 - 1):
        blocks.append((0, 2 * i + 2, far[i].at[0]))
    for k in range(2, groups):
        blocks.append((1, k, far[groups // 2 - 1 + k - 2].at[...]))
    for i, k, beam_ref in blocks:
        values = beam_ref[...].astype(F32)
        start = (me ^ k) * dishes
        for f in range(chans):
            for b in range(group_beams):
                for part in range(2):
                    first = (f * group_beams + b) * block + part * dishes
                    gathered[
                        (i * pairs + b * chans + f) * 2 + part,
                        pl.ds(start, dishes),
                        :,
                    ] = values[first : first + dishes]
    for pair in range(pairs):
        total = None
        for i in range(cycles):
            real = gathered[(i * pairs + pair) * 2]
            imag = gathered[(i * pairs + pair) * 2 + 1]
            top = jnp.concatenate([real, imag], axis=1)
            left = jnp.concatenate([top, jnp.concatenate([imag, -real], axis=1)]).astype(BF16)
            right = jnp.concatenate(
                [top, jnp.zeros((samples - pad_dishes, 2 * samples), F32)]
            ).astype(BF16)
            term = dot_t(left, right)
            total = term if total is None else total + term
        sums[pl.ds(pair, 2 * pad_dishes, stride=pad_pairs), :] = total * scale
    for part in range(2):
        pieces = []
        for d in range(all_dishes):
            first = (part * pad_dishes + d) * pad_pairs
            pieces.append(sums[first : first + pad_pairs, 0:all_dishes])
        flat = jnp.concatenate(pieces, axis=1)
        for b in range(group_beams):
            out_ref[part, b] = flat[b * chans : (b + 1) * chans]


def vmem():
    return pl.BlockSpec(memory_space=pltpu.VMEM)


def smem():
    return pl.BlockSpec(memory_space=pltpu.SMEM)


def per_device(voltages, weights, sat_index, offsets, angles):
    cycles, _, dishes, chans, ports, samples = voltages.shape
    beams = weights.shape[3]
    slots = sat_index.shape[2]
    groups = lax.axis_size("section")
    peers = lax.axis_size("chan")
    group_beams = beams // groups
    pad_beams = rounded_up(beams)
    assert cycles == 2 and chans == 2 and sat_index.shape[1] == 1
    assert groups > 1 and groups & (groups - 1) == 0
    dims = (groups, chans, group_beams, dishes, pad_beams)
    wide = ports * chans
    x = voltages.transpose(0, 1, 2, 4, 3, 5).reshape(cycles, 2, dishes, wide, samples)

    def swap(value, first):
        path = []
        for i in range(peers):
            other = i + 1 if i % 2 == first else i - 1
            for q in range(groups):
                to = other * groups + q if 0 <= other < peers else i * groups + (q ^ 1)
                path.append((i * groups + q, to))
        return lax.ppermute(value, ("chan", "section"), path)

    def params(**more):
        return pltpu.CompilerParams(vmem_limit_bytes=VMEM_GRANT, **more)

    def step_over(value, step):
        return lax.ppermute(value, "section", [(i, i ^ step) for i in range(groups)])

    sat_b = swap(sat_index, 1)
    sat_a = swap(sat_index, 0)

    chunk = 2 * chans * group_beams * dishes
    piece = jax.ShapeDtypeStruct((chunk, samples), BF16)
    two = jax.ShapeDtypeStruct((2, chunk, samples), BF16)
    several = jax.ShapeDtypeStruct((groups // 2 + 1, chunk, samples), BF16)
    stage = pltpu.VMEM((groups * stage_rows(dims), samples), F32)

    first_near, first_mine, *first_far = pl.pallas_call(
        functools.partial(first_beams_kernel, dims),
        out_shape=(piece, piece) + (two,) * (groups // 2 - 1),
        in_specs=[pl.BlockSpec(memory_space=pltpu.HBM), vmem()],
        out_specs=(vmem(),) * (groups // 2 + 1),
        scratch_shapes=[
            stage,
            pltpu.VMEM((2, dishes, wide, samples), BF16),
            pltpu.SemaphoreType.DMA((dishes,)),
        ],
        compiler_params=params(),
        name="first_beams",
    )(pltpu.with_memory_space_constraint(x, pltpu.HBM), weights)
    first_got = [step_over(value, 2 * i + 2) for i, value in enumerate(first_far)]

    rows = chans * 2 * slots
    vectors = jax.ShapeDtypeStruct((cycles, dishes, 2 * slots, ports), F32)
    own, to_a, to_b = pl.pallas_call(
        nulls_kernel,
        out_shape=(vectors,) * 3,
        in_specs=[smem(), smem(), smem(), vmem(), vmem(), vmem()],
        out_specs=(vmem(),) * 3,
        scratch_shapes=[
            pltpu.VMEM((cycles * rows, ports), F32),
            pltpu.VMEM((cycles * dishes * 2 * rows, wide), F32),
        ],
        compiler_params=params(),
        name="nulls",
    )(sat_index[:, 0], sat_a[:, 0], sat_b[:, 0], offsets, angles, x)
    from_b = swap(to_b, 1)
    from_a = swap(to_a, 0)

    next_rows = jax.ShapeDtypeStruct((dishes, 2 * chans * pad_beams, ports), BF16)
    second_near, second_mine, *second_far, w_next = pl.pallas_call(
        functools.partial(next_beams_kernel, dims, 0),
        out_shape=(several, piece) + (piece,) * (groups - 2) + (next_rows,),
        in_specs=[vmem()] * (5 + groups // 2),
        out_specs=(vmem(),) * (groups + 1),
        scratch_shapes=[stage],
        compiler_params=params(),
        name="next_beams",
    )(x, weights, own, from_a, from_b, first_near, *first_got)
    second_got = [step_over(value, k + 2) for k, value in enumerate(second_far)]
    near_got = step_over(second_near, 1)

    new_weights = pl.pallas_call(
        functools.partial(last_nulls_kernel, dims, 1),
        out_shape=jax.ShapeDtypeStruct(weights.shape, BF16),
        in_specs=[vmem()] * 4,
        out_specs=vmem(),
        compiler_params=params(),
        name="last_nulls",
    )(w_next, own, from_a, from_b)

    all_dishes = dishes * groups
    pairs = group_beams * chans
    pad_dishes = rounded_up(all_dishes)
    vis = pl.pallas_call(
        functools.partial(correlate_kernel, dims, 1.0 / (cycles * samples)),
        out_shape=jax.ShapeDtypeStruct((2, group_beams, chans, all_dishes * all_dishes), F32),
        in_specs=[vmem()] * (3 + groups // 2 - 1 + groups - 2),
        out_specs=vmem(),
        scratch_shapes=[
            pltpu.VMEM((cycles * pairs * 2, pad_dishes, samples), F32),
            pltpu.VMEM((2 * pad_dishes * rounded_up(pairs), samples), F32),
        ],
        compiler_params=params(),
        name="correlate",
    )(first_mine, second_mine, near_got, *first_got, *second_got)
    return vis, new_weights


def solution(mesh):
    placed = (
        P(None, None, "section", "chan", None, None),
        P(None, "section", "chan", None, None),
        P(None, "chan", None),
        P(),
        P(),
    )
    return jax.shard_map(
        per_device,
        mesh=mesh,
        in_specs=placed,
        out_specs=(P(None, "section", "chan", None), P(None, "section", "chan", None, None)),
        check_vma=False,
    )
```

```python
import functools

import jax
import jax.numpy as jnp
from jax import lax
from jax.experimental import pallas as pl
from jax.experimental.pallas import tpu as pltpu
from jax.sharding import PartitionSpec as P


LOADING = 100.0
F32 = jnp.float32
BF16 = jnp.bfloat16
SUB = 8
VMEM_GRANT = 20 * 1024 * 1024


def rounded_up(size):
    return -(-size // SUB) * SUB


def spread_matrix(ports, chans):
    port = lax.broadcasted_iota(jnp.int32, (ports, ports * chans), 0) * chans
    lane = lax.broadcasted_iota(jnp.int32, (ports, ports * chans), 1)
    return jnp.where((lane >= port) & (lane < port + chans), 1.0, 0.0).astype(BF16)


def own_channel(rows, rows_per_chan, ports, chans):
    row = lax.broadcasted_iota(jnp.int32, (rows, ports * chans), 0)
    lane = lax.broadcasted_iota(jnp.int32, (rows, ports * chans), 1)
    return lax.rem(lax.div(row, rows_per_chan), chans) == lax.rem(lane, chans)


def split(value):
    high = value.astype(BF16)
    low = (value - high.astype(F32)).astype(BF16)
    return high, low


def dot(left, right):
    return jnp.dot(left, right, preferred_element_type=F32)


def dot_t(left, right):
    return lax.dot_general(left, right, (((1,), (1,)), ((), ())), preferred_element_type=F32)


def spread_rows(weight_rows, spread, keep):
    wide = jnp.where(keep, dot(weight_rows, spread), 0.0)
    half = wide.shape[0] // 2
    real, imag = wide[:half], wide[half:]
    on_real = jnp.concatenate([real, -imag]).astype(BF16)
    on_imag = jnp.concatenate([imag, real]).astype(BF16)
    return on_real, on_imag


def beams_of(weight_rows, spread, keep, x_real, x_imag):
    on_real, on_imag = spread_rows(weight_rows, spread, keep)
    return dot(on_real, x_real) + dot(on_imag, x_imag)


def put_beams(beam_rows, stage, dish, dims):
    groups, chans, group_beams, dishes, pad_beams = dims
    block = 2 * dishes
    for part in range(2):
        for f in range(chans):
            for g in range(groups):
                source = (part * chans + f) * pad_beams + g * group_beams
                first = g * stage_rows(dims) + f * group_beams * block + part * dishes + dish
                stage[pl.ds(first, group_beams, stride=block), :] = beam_rows[
                    source : source + group_beams
                ]


def stage_rows(dims):
    _, chans, group_beams, dishes, _ = dims
    return rounded_up(chans * group_beams * 2 * dishes)


def flush_beams(stage, outs, steps, dims):
    me = lax.axis_index("section")
    rows = outs[0].shape[0]
    for k, out in zip(steps, outs):
        first = pl.multiple_of((me ^ k) * stage_rows(dims), SUB)
        out[...] = stage[pl.ds(first, stage_rows(dims)), :][:rows].astype(BF16)


def weight_rows_of(w_ref, d, pad_beams):
    parts, _, chans, beams, ports = w_ref.shape
    pieces = []
    for part in range(parts):
        for f in range(chans):
            pieces.append(w_ref[part, d, f].astype(F32))
            if pad_beams > beams:
                pieces.append(jnp.zeros((pad_beams - beams, ports), F32))
    return jnp.concatenate(pieces)


def spread_kernel(dims, w_ref, out_ref):
    chans, pad_beams = dims[1], dims[4]
    ports = w_ref.shape[-1]
    spread = spread_matrix(ports, chans)
    keep = own_channel(2 * chans * pad_beams, pad_beams, ports, chans)
    for d in range(w_ref.shape[1]):
        rows = weight_rows_of(w_ref, d, pad_beams).astype(BF16)
        out_ref[d, 0], out_ref[d, 1] = spread_rows(rows, spread, keep)


def first_beams_kernel(dims, x_ref, wide_ref, *refs):
    (near, mine, *far), stage = refs[:-1], refs[-1]
    for d in range(x_ref.shape[2]):
        rows = dot(wide_ref[d, 0], x_ref[0, 0, d]) + dot(wide_ref[d, 1], x_ref[0, 1, d])
        put_beams(rows, stage, d, dims)
    flush_beams(stage, [mine, near], [0, 1], dims)
    for i, out in enumerate(far):
        flush_beams(stage, [out.at[0], out.at[1]], [2 * i + 2, 2 * i + 3], dims)


def even_place():
    return lax.rem(lax.axis_index("chan"), 2) == 0


def nulls_kernel(sat_ref, sat_a_ref, sat_b_ref, off_ref, ang_ref, x_ref,
                 own_ref, a_ref, b_ref, phase, folded):
    cycles, _, dishes, wide, samples = x_ref.shape
    ports = ang_ref.shape[-1]
    chans = wide // ports
    slots = sat_ref.shape[-1]
    per_chan = 2 * slots
    rows = chans * per_chan
    spread = spread_matrix(ports, chans)
    even = even_place()
    place = lax.axis_index("chan")
    last_place = lax.axis_size("chan") - 1
    time = lax.broadcasted_iota(jnp.int32, (samples, off_ref.shape[1]), 0)
    ones = jnp.ones((rows, off_ref.shape[1]), BF16)
    for c in range(cycles):
        for f in range(chans):
            swapped = even if f == 0 else jnp.logical_not(even)
            for s in range(slots):
                base = f * per_chan + s
                phase[pl.ds(c * rows + base, 1), :] = ang_ref[pl.ds(sat_ref[c, s], 1), :]
                phase[pl.ds(c * rows + base + slots, 1), :] = ang_ref[
                    pl.ds(jnp.where(swapped, sat_b_ref[c, s], sat_a_ref[c, s]), 1), :
                ]
    angle = phase[...]
    cosine, sine = jnp.cos(angle), jnp.sin(angle)
    keep4 = own_channel(4 * rows, per_chan, ports, chans)
    keep2 = own_channel(2 * rows, per_chan, ports, chans)
    for c in range(cycles):
        hits = jnp.where(time == off_ref[c : c + 1, :], 1.0, 0.0).astype(BF16)
        counts = dot_t(ones, hits)
        a_real = cosine[c * rows : (c + 1) * rows]
        a_imag = sine[c * rows : (c + 1) * rows]
        real_h, real_l = split(a_real)
        imag_h, imag_l = split(a_imag)
        column = jnp.concatenate(
            [real_h.astype(F32), real_l.astype(F32), imag_h.astype(F32), imag_l.astype(F32)]
        ).astype(BF16)
        wide_rows = jnp.where(keep4, dot(column, spread), 0.0)
        half = 2 * rows
        on_real = wide_rows.astype(BF16)
        on_imag = jnp.concatenate([wide_rows[half:], -wide_rows[:half]]).astype(BF16)
        for d in range(dishes):
            x_real, x_imag = x_ref[c, 0, d], x_ref[c, 1, d]
            inner = dot(on_real, x_real) + dot(on_imag, x_imag)
            inner_real = (inner[0:rows] + inner[rows:half]) * counts
            inner_imag = (inner[half : half + rows] + inner[half + rows :]) * counts
            real_h, real_l = split(inner_real)
            imag_h, imag_l = split(inner_imag)
            pieces = jnp.concatenate(
                [real_h.astype(F32), real_l.astype(F32), imag_h.astype(F32), imag_l.astype(F32)]
            )
            turned = jnp.concatenate([-pieces[half:], pieces[:half]])
            outer = dot_t(pieces.astype(BF16), x_real) + dot_t(turned.astype(BF16), x_imag)
            both = jnp.concatenate(
                [outer[0:rows] + outer[rows:half], outer[half : half + rows] + outer[half + rows :]]
            )
            first = (c * dishes + d) * 2 * rows
            folded[first : first + 2 * rows, :] = jnp.where(keep2, both, 0.0)
    high, low = split(folded[...])
    summed = dot_t(high, spread) + dot_t(low, spread)
    for c in range(cycles):
        for d in range(dishes):
            first = (c * dishes + d) * 2 * rows
            for part in range(2):
                block = summed[first + part * rows : first + (part + 1) * rows]
                own = block[0:slots]
                for f in range(1, chans):
                    own = own + block[f * per_chan : f * per_chan + slots]
                along = (cosine if part == 0 else sine)[c * rows : c * rows + slots]
                last = (chans - 1) * per_chan + slots
                where = slice(part * slots, (part + 1) * slots)
                own_ref[c, d, where, :] = own + LOADING * along
                to_dn = jnp.where(place > 0, block[slots : 2 * slots], 0.0)
                to_up = jnp.where(place < last_place, block[last : last + slots], 0.0)
                a_ref[c, d, where, :] = jnp.where(even, to_up, to_dn)
                b_ref[c, d, where, :] = jnp.where(even, to_dn, to_up)


def null_rows(rows, own, beside, chans, pad_beams):
    slots = own.shape[0] // 2
    half = rows.shape[0] // 2
    reals, imags = [], []
    for f in range(chans):
        real = rows[f * pad_beams : (f + 1) * pad_beams]
        imag = rows[half + f * pad_beams : half + (f + 1) * pad_beams]
        null = own + beside[f]
        for s in range(slots):
            u_real = null[s : s + 1]
            u_imag = null[slots + s : slots + s + 1]
            inverse = 1.0 / jnp.sum(u_real * u_real + u_imag * u_imag, axis=-1, keepdims=True)
            c_real = jnp.sum(real * u_real + imag * u_imag, axis=-1, keepdims=True) * inverse
            c_imag = jnp.sum(imag * u_real - real * u_imag, axis=-1, keepdims=True) * inverse
            real = real - (u_real * c_real - u_imag * c_imag)
            imag = imag - (u_real * c_imag + u_imag * c_real)
        reals.append(real)
        imags.append(imag)
    return jnp.concatenate(reals + imags)


def beside_of(a_ref, b_ref, cycle, d):
    even = even_place()
    a, b = a_ref[cycle, d], b_ref[cycle, d]
    return jnp.where(even, b, a), jnp.where(even, a, b)


def next_beams_kernel(dims, cycle, x_ref, w_ref, own_ref, a_ref, b_ref, near_ref, *refs):
    groups = dims[0]
    passed, (near, mine, *far), (next_ref, stage) = refs[: groups // 2 - 1], refs[groups // 2 - 1 : -2], refs[-2:]
    near[0] = near_ref[...]
    for i, passed_ref in enumerate(passed):
        near[i + 1] = passed_ref[1]
    dishes = x_ref.shape[2]
    chans, pad_beams = dims[1], dims[4]
    ports = w_ref.shape[-1]
    spread = spread_matrix(ports, chans)
    keep = own_channel(2 * chans * pad_beams, pad_beams, ports, chans)
    for d in range(dishes):
        rows = null_rows(
            weight_rows_of(w_ref, d, pad_beams),
            own_ref[cycle, d],
            beside_of(a_ref, b_ref, cycle, d),
            chans,
            pad_beams,
        ).astype(BF16)
        next_ref[d] = rows
        put_beams(
            beams_of(rows, spread, keep, x_ref[cycle + 1, 0, d], x_ref[cycle + 1, 1, d]),
            stage,
            d,
            dims,
        )
    flush_beams(stage, [mine, near.at[groups // 2], *far], range(groups), dims)


def last_nulls_kernel(dims, cycle, w_ref, own_ref, a_ref, b_ref, out_ref):
    chans, pad_beams = dims[1], dims[4]
    beams = out_ref.shape[3]
    for d in range(w_ref.shape[0]):
        rows = null_rows(
            w_ref[d].astype(F32),
            own_ref[cycle, d],
            beside_of(a_ref, b_ref, cycle, d),
            chans,
            pad_beams,
        )
        for part in range(2):
            for f in range(chans):
                first = (part * chans + f) * pad_beams
                out_ref[part, d, f] = rows[first : first + beams].astype(BF16)


def correlate_kernel(dims, scale, *refs):
    groups, chans, group_beams, dishes, _ = dims
    beam_refs, out_ref, gathered, sums = refs[:-3], refs[-3], refs[-2], refs[-1]
    all_dishes = groups * dishes
    pad_dishes = rounded_up(all_dishes)
    pairs = group_beams * chans
    pad_pairs = rounded_up(pairs)
    samples = gathered.shape[-1]
    block = 2 * dishes
    filler = jnp.zeros((pad_dishes, samples), F32)
    for i in range(gathered.shape[0]):
        gathered[i] = filler
    me = lax.axis_index("section")
    cycles = 2
    mine, near, far = beam_refs[:2], beam_refs[2], beam_refs[3:]
    blocks = [(0, 0, mine[0].at[...]), (1, 0, mine[1].at[...])]
    for i in range(groups // 2):
        blocks.append((0, 2 * i + 1, near.at[i]))
    blocks.append((1, 1, near.at[groups // 2]))
    for i in range(groups // 2 - 1):
        blocks.append((0, 2 * i + 2, far[i].at[0]))
    for k in range(2, groups):
        blocks.append((1, k, far[groups // 2 - 1 + k - 2].at[...]))
    for i, k, beam_ref in blocks:
        values = beam_ref[...].astype(F32)
        start = (me ^ k) * dishes
        for f in range(chans):
            for b in range(group_beams):
                for part in range(2):
                    first = (f * group_beams + b) * block + part * dishes
                    gathered[
                        (i * pairs + b * chans + f) * 2 + part,
                        pl.ds(start, dishes),
                        :,
                    ] = values[first : first + dishes]
    for pair in range(pairs):
        total = None
        for i in range(cycles):
            real = gathered[(i * pairs + pair) * 2]
            imag = gathered[(i * pairs + pair) * 2 + 1]
            top = jnp.concatenate([real, imag], axis=1)
            left = jnp.concatenate([top, jnp.concatenate([imag, -real], axis=1)]).astype(BF16)
            right = jnp.concatenate(
                [top, jnp.zeros((samples - pad_dishes, 2 * samples), F32)]
            ).astype(BF16)
            term = dot_t(left, right)
            total = term if total is None else total + term
        sums[pl.ds(pair, 2 * pad_dishes, stride=pad_pairs), :] = total * scale
    for part in range(2):
        pieces = []
        for d in range(all_dishes):
            first = (part * pad_dishes + d) * pad_pairs
            pieces.append(sums[first : first + pad_pairs, 0:all_dishes])
        flat = jnp.concatenate(pieces, axis=1)
        for b in range(group_beams):
            out_ref[part, b] = flat[b * chans : (b + 1) * chans]


def vmem():
    return pl.BlockSpec(memory_space=pltpu.VMEM)


def smem():
    return pl.BlockSpec(memory_space=pltpu.SMEM)


def per_device(voltages, weights, sat_index, offsets, angles):
    cycles, _, dishes, chans, ports, samples = voltages.shape
    beams = weights.shape[3]
    slots = sat_index.shape[2]
    groups = lax.axis_size("section")
    peers = lax.axis_size("chan")
    group_beams = beams // groups
    pad_beams = rounded_up(beams)
    assert cycles == 2 and chans == 2 and sat_index.shape[1] == 1
    assert groups > 1 and groups & (groups - 1) == 0
    dims = (groups, chans, group_beams, dishes, pad_beams)
    wide = ports * chans
    x = voltages.transpose(0, 1, 2, 4, 3, 5).reshape(cycles, 2, dishes, wide, samples)

    def swap(value, first):
        path = []
        for i in range(peers):
            other = i + 1 if i % 2 == first else i - 1
            for q in range(groups):
                to = other * groups + q if 0 <= other < peers else i * groups + (q ^ 1)
                path.append((i * groups + q, to))
        return lax.ppermute(value, ("chan", "section"), path)

    def params(**more):
        return pltpu.CompilerParams(vmem_limit_bytes=VMEM_GRANT, **more)

    def step_over(value, step):
        return lax.ppermute(value, "section", [(i, i ^ step) for i in range(groups)])

    sat_b = swap(sat_index, 1)
    sat_a = swap(sat_index, 0)

    chunk = 2 * chans * group_beams * dishes
    piece = jax.ShapeDtypeStruct((chunk, samples), BF16)
    two = jax.ShapeDtypeStruct((2, chunk, samples), BF16)
    several = jax.ShapeDtypeStruct((groups // 2 + 1, chunk, samples), BF16)
    stage = pltpu.VMEM((groups * stage_rows(dims), samples), F32)

    wide_rows = pl.pallas_call(
        functools.partial(spread_kernel, dims),
        out_shape=jax.ShapeDtypeStruct((dishes, 2, 2 * chans * pad_beams, wide), BF16),
        in_specs=[vmem()],
        out_specs=vmem(),
        compiler_params=params(),
        name="spread",
    )(weights)
    first_near, first_mine, *first_far = pl.pallas_call(
        functools.partial(first_beams_kernel, dims),
        out_shape=(piece, piece) + (two,) * (groups // 2 - 1),
        in_specs=[vmem()] * 2,
        out_specs=(vmem(),) * (groups // 2 + 1),
        scratch_shapes=[stage],
        compiler_params=params(),
        name="first_beams",
    )(x, wide_rows)
    first_got = [step_over(value, 2 * i + 2) for i, value in enumerate(first_far)]

    rows = chans * 2 * slots
    vectors = jax.ShapeDtypeStruct((cycles, dishes, 2 * slots, ports), F32)
    own, to_a, to_b = pl.pallas_call(
        nulls_kernel,
        out_shape=(vectors,) * 3,
        in_specs=[smem(), smem(), smem(), vmem(), vmem(), vmem()],
        out_specs=(vmem(),) * 3,
        scratch_shapes=[
            pltpu.VMEM((cycles * rows, ports), F32),
            pltpu.VMEM((cycles * dishes * 2 * rows, wide), F32),
        ],
        compiler_params=params(),
        name="nulls",
    )(sat_index[:, 0], sat_a[:, 0], sat_b[:, 0], offsets, angles, x)
    from_b = swap(to_b, 1)
    from_a = swap(to_a, 0)

    next_rows = jax.ShapeDtypeStruct((dishes, 2 * chans * pad_beams, ports), BF16)
    second_near, second_mine, *second_far, w_next = pl.pallas_call(
        functools.partial(next_beams_kernel, dims, 0),
        out_shape=(several, piece) + (piece,) * (groups - 2) + (next_rows,),
        in_specs=[vmem()] * (5 + groups // 2),
        out_specs=(vmem(),) * (groups + 1),
        scratch_shapes=[stage],
        compiler_params=params(),
        name="next_beams",
    )(x, weights, own, from_a, from_b, first_near, *first_got)
    second_got = [step_over(value, k + 2) for k, value in enumerate(second_far)]
    near_got = step_over(second_near, 1)

    new_weights = pl.pallas_call(
        functools.partial(last_nulls_kernel, dims, 1),
        out_shape=jax.ShapeDtypeStruct(weights.shape, BF16),
        in_specs=[vmem()] * 4,
        out_specs=vmem(),
        compiler_params=params(),
        name="last_nulls",
    )(w_next, own, from_a, from_b)

    all_dishes = dishes * groups
    pairs = group_beams * chans
    pad_dishes = rounded_up(all_dishes)
    vis = pl.pallas_call(
        functools.partial(correlate_kernel, dims, 1.0 / (cycles * samples)),
        out_shape=jax.ShapeDtypeStruct((2, group_beams, chans, all_dishes * all_dishes), F32),
        in_specs=[vmem()] * (3 + groups // 2 - 1 + groups - 2),
        out_specs=vmem(),
        scratch_shapes=[
            pltpu.VMEM((cycles * pairs * 2, pad_dishes, samples), F32),
            pltpu.VMEM((2 * pad_dishes * rounded_up(pairs), samples), F32),
        ],
        compiler_params=params(),
        name="correlate",
    )(first_mine, second_mine, near_got, *first_got, *second_got)
    return vis, new_weights


def solution(mesh):
    placed = (
        P(None, None, "section", "chan", None, None),
        P(None, "section", "chan", None, None),
        P(None, "chan", None),
        P(),
        P(),
    )
    return jax.shard_map(
        per_device,
        mesh=mesh,
        in_specs=placed,
        out_specs=(P(None, "section", "chan", None), P(None, "section", "chan", None, None)),
        check_vma=False,
    )
```

```python
import functools

import jax
import jax.numpy as jnp
from jax import lax
from jax.experimental import pallas as pl
from jax.experimental.pallas import tpu as pltpu
from jax.sharding import PartitionSpec as P


LOADING = 100.0
F32 = jnp.float32
BF16 = jnp.bfloat16
SUB = 8
VMEM_GRANT = 20 * 1024 * 1024


def rounded_up(size):
    return -(-size // SUB) * SUB


def spread_matrix(ports, chans):
    port = lax.broadcasted_iota(jnp.int32, (ports, ports * chans), 0) * chans
    lane = lax.broadcasted_iota(jnp.int32, (ports, ports * chans), 1)
    return jnp.where((lane >= port) & (lane < port + chans), 1.0, 0.0).astype(BF16)


def own_channel(rows, rows_per_chan, ports, chans):
    row = lax.broadcasted_iota(jnp.int32, (rows, ports * chans), 0)
    lane = lax.broadcasted_iota(jnp.int32, (rows, ports * chans), 1)
    return lax.rem(lax.div(row, rows_per_chan), chans) == lax.rem(lane, chans)


def split(value):
    high = value.astype(BF16)
    low = (value - high.astype(F32)).astype(BF16)
    return high, low


def dot(left, right):
    return jnp.dot(left, right, preferred_element_type=F32)


def dot_t(left, right):
    return lax.dot_general(left, right, (((1,), (1,)), ((), ())), preferred_element_type=F32)


def spread_rows(weight_rows, spread, keep):
    wide = jnp.where(keep, dot(weight_rows, spread), 0.0)
    half = wide.shape[0] // 2
    real, imag = wide[:half], wide[half:]
    on_real = jnp.concatenate([real, -imag]).astype(BF16)
    on_imag = jnp.concatenate([imag, real]).astype(BF16)
    return on_real, on_imag


def beams_of(weight_rows, spread, keep, x_real, x_imag):
    on_real, on_imag = spread_rows(weight_rows, spread, keep)
    return dot(on_real, x_real) + dot(on_imag, x_imag)


def put_beams(beam_rows, stage, dish, dims):
    groups, chans, group_beams, dishes, pad_beams = dims
    block = 2 * dishes
    for part in range(2):
        for f in range(chans):
            for g in range(groups):
                source = (part * chans + f) * pad_beams + g * group_beams
                first = g * stage_rows(dims) + f * group_beams * block + part * dishes + dish
                stage[pl.ds(first, group_beams, stride=block), :] = beam_rows[
                    source : source + group_beams
                ]


def stage_rows(dims):
    _, chans, group_beams, dishes, _ = dims
    return rounded_up(chans * group_beams * 2 * dishes)


def flush_beams(stage, outs, steps, dims):
    me = lax.axis_index("section")
    rows = outs[0].shape[0]
    for k, out in zip(steps, outs):
        first = pl.multiple_of((me ^ k) * stage_rows(dims), SUB)
        out[...] = stage[pl.ds(first, stage_rows(dims)), :][:rows].astype(BF16)


def weight_rows_of(w_ref, d, pad_beams):
    parts, _, chans, beams, ports = w_ref.shape
    pieces = []
    for part in range(parts):
        for f in range(chans):
            pieces.append(w_ref[part, d, f].astype(F32))
            if pad_beams > beams:
                pieces.append(jnp.zeros((pad_beams - beams, ports), F32))
    return jnp.concatenate(pieces)


def spread_kernel(dims, w_ref, out_ref):
    chans, pad_beams = dims[1], dims[4]
    ports = w_ref.shape[-1]
    spread = spread_matrix(ports, chans)
    keep = own_channel(2 * chans * pad_beams, pad_beams, ports, chans)
    for d in range(w_ref.shape[1]):
        rows = weight_rows_of(w_ref, d, pad_beams).astype(BF16)
        out_ref[d, 0], out_ref[d, 1] = spread_rows(rows, spread, keep)


def first_beams_kernel(dims, x_ref, wide_ref, *refs):
    (near, mine, *far), stage = refs[:-1], refs[-1]
    for d in range(x_ref.shape[2]):
        rows = dot(wide_ref[d, 0], x_ref[0, 0, d]) + dot(wide_ref[d, 1], x_ref[0, 1, d])
        put_beams(rows, stage, d, dims)
    flush_beams(stage, [mine, near], [0, 1], dims)
    for i, out in enumerate(far):
        flush_beams(stage, [out.at[0], out.at[1]], [2 * i + 2, 2 * i + 3], dims)


def even_place():
    return lax.rem(lax.axis_index("chan"), 2) == 0


def stacked_halves(real, imag):
    real_h, real_l = split(real)
    imag_h, imag_l = split(imag)
    return jnp.concatenate(
        [real_h.astype(F32), real_l.astype(F32), imag_h.astype(F32), imag_l.astype(F32)]
    )


def nulls_kernel(cycle, sat_ref, sat_a_ref, sat_b_ref, off_ref, ang_ref, x_ref,
                 own_ref, a_ref, b_ref, phase, inner, folded):
    _, _, dishes, wide, samples = x_ref.shape
    ports = ang_ref.shape[-1]
    chans = wide // ports
    slots = sat_ref.shape[-1]
    per_chan = 2 * slots
    rows = chans * per_chan
    half = 2 * rows
    spread = spread_matrix(ports, chans)
    even = even_place()
    place = lax.axis_index("chan")
    last_place = lax.axis_size("chan") - 1
    for f in range(chans):
        swapped = even if f == 0 else jnp.logical_not(even)
        for s in range(slots):
            base = f * per_chan + s
            beside = jnp.where(swapped, sat_b_ref[cycle, s], sat_a_ref[cycle, s])
            phase[pl.ds(base, 1), :] = ang_ref[pl.ds(sat_ref[cycle, s], 1), :]
            phase[pl.ds(base + slots, 1), :] = ang_ref[pl.ds(beside, 1), :]
    cosine, sine = jnp.cos(phase[...]), jnp.sin(phase[...])
    time = lax.broadcasted_iota(jnp.int32, (samples, off_ref.shape[1]), 0)
    hits = jnp.where(time == off_ref[cycle : cycle + 1, :], 1.0, 0.0).astype(BF16)
    counts = dot_t(jnp.ones((rows, off_ref.shape[1]), BF16), hits)
    column = stacked_halves(cosine, sine).astype(BF16)
    keep4 = own_channel(4 * rows, per_chan, ports, chans)
    wide_rows = jnp.where(keep4, dot(column, spread), 0.0)
    on_real = wide_rows.astype(BF16)
    on_imag = jnp.concatenate([wide_rows[half:], -wide_rows[:half]]).astype(BF16)
    for d in range(dishes):
        inner[d] = dot(on_real, x_ref[cycle, 0, d]) + dot(on_imag, x_ref[cycle, 1, d])
    keep2 = own_channel(2 * rows, per_chan, ports, chans)
    for d in range(dishes):
        now = inner[d]
        pieces = stacked_halves(
            (now[0:rows] + now[rows:half]) * counts,
            (now[half : half + rows] + now[half + rows :]) * counts,
        )
        turned = jnp.concatenate([-pieces[half:], pieces[:half]])
        outer = dot_t(pieces.astype(BF16), x_ref[cycle, 0, d]) + dot_t(
            turned.astype(BF16), x_ref[cycle, 1, d]
        )
        both = jnp.concatenate(
            [outer[0:rows] + outer[rows:half], outer[half : half + rows] + outer[half + rows :]]
        )
        folded[d * half : (d + 1) * half, :] = jnp.where(keep2, both, 0.0)
    high, low = split(folded[...])
    summed = dot_t(high, spread) + dot_t(low, spread)
    for d in range(dishes):
        for part in range(2):
            first = (2 * d + part) * rows
            block = summed[first : first + rows]
            own = block[0:slots]
            for f in range(1, chans):
                own = own + block[f * per_chan : f * per_chan + slots]
            along = (cosine if part == 0 else sine)[0:slots]
            last = (chans - 1) * per_chan + slots
            where = slice(part * slots, (part + 1) * slots)
            own_ref[d, where, :] = own + LOADING * along
            to_dn = jnp.where(place > 0, block[slots : 2 * slots], 0.0)
            to_up = jnp.where(place < last_place, block[last : last + slots], 0.0)
            a_ref[d, where, :] = jnp.where(even, to_up, to_dn)
            b_ref[d, where, :] = jnp.where(even, to_dn, to_up)


def null_rows(rows, own, beside, chans, pad_beams):
    slots = own.shape[0] // 2
    half = rows.shape[0] // 2
    reals, imags = [], []
    for f in range(chans):
        real = rows[f * pad_beams : (f + 1) * pad_beams]
        imag = rows[half + f * pad_beams : half + (f + 1) * pad_beams]
        null = own + beside[f]
        for s in range(slots):
            u_real = null[s : s + 1]
            u_imag = null[slots + s : slots + s + 1]
            inverse = 1.0 / jnp.sum(u_real * u_real + u_imag * u_imag, axis=-1, keepdims=True)
            c_real = jnp.sum(real * u_real + imag * u_imag, axis=-1, keepdims=True) * inverse
            c_imag = jnp.sum(imag * u_real - real * u_imag, axis=-1, keepdims=True) * inverse
            real = real - (u_real * c_real - u_imag * c_imag)
            imag = imag - (u_real * c_imag + u_imag * c_real)
        reals.append(real)
        imags.append(imag)
    return jnp.concatenate(reals + imags)


def beside_of(a_ref, b_ref, d):
    even = even_place()
    a, b = a_ref[d], b_ref[d]
    return jnp.where(even, b, a), jnp.where(even, a, b)


def next_beams_kernel(dims, cycle, x_ref, w_ref, own_ref, a_ref, b_ref, near_ref, *refs):
    groups = dims[0]
    passed, (near, mine, *far), (next_ref, stage) = refs[: groups // 2 - 1], refs[groups // 2 - 1 : -2], refs[-2:]
    near[0] = near_ref[...]
    for i, passed_ref in enumerate(passed):
        near[i + 1] = passed_ref[1]
    dishes = x_ref.shape[2]
    chans, pad_beams = dims[1], dims[4]
    ports = w_ref.shape[-1]
    spread = spread_matrix(ports, chans)
    keep = own_channel(2 * chans * pad_beams, pad_beams, ports, chans)
    for d in range(dishes):
        rows = null_rows(
            weight_rows_of(w_ref, d, pad_beams),
            own_ref[d],
            beside_of(a_ref, b_ref, d),
            chans,
            pad_beams,
        ).astype(BF16)
        next_ref[d] = rows
        put_beams(
            beams_of(rows, spread, keep, x_ref[cycle + 1, 0, d], x_ref[cycle + 1, 1, d]),
            stage,
            d,
            dims,
        )
    flush_beams(stage, [mine, near.at[groups // 2], *far], range(groups), dims)


def last_nulls_kernel(dims, w_ref, own_ref, a_ref, b_ref, out_ref):
    chans, pad_beams = dims[1], dims[4]
    beams = out_ref.shape[3]
    for d in range(w_ref.shape[0]):
        rows = null_rows(
            w_ref[d].astype(F32),
            own_ref[d],
            beside_of(a_ref, b_ref, d),
            chans,
            pad_beams,
        )
        for part in range(2):
            for f in range(chans):
                first = (part * chans + f) * pad_beams
                out_ref[part, d, f] = rows[first : first + beams].astype(BF16)


def correlate_kernel(dims, scale, *refs):
    groups, chans, group_beams, dishes, _ = dims
    beam_refs, out_ref, gathered, sums = refs[:-3], refs[-3], refs[-2], refs[-1]
    all_dishes = groups * dishes
    pad_dishes = rounded_up(all_dishes)
    pairs = group_beams * chans
    pad_pairs = rounded_up(pairs)
    samples = gathered.shape[-1]
    block = 2 * dishes
    filler = jnp.zeros((pad_dishes, samples), F32)
    for i in range(gathered.shape[0]):
        gathered[i] = filler
    me = lax.axis_index("section")
    cycles = 2
    mine, near, far = beam_refs[:2], beam_refs[2], beam_refs[3:]
    blocks = [(0, 0, mine[0].at[...]), (1, 0, mine[1].at[...])]
    for i in range(groups // 2):
        blocks.append((0, 2 * i + 1, near.at[i]))
    blocks.append((1, 1, near.at[groups // 2]))
    for i in range(groups // 2 - 1):
        blocks.append((0, 2 * i + 2, far[i].at[0]))
    for k in range(2, groups):
        blocks.append((1, k, far[groups // 2 - 1 + k - 2].at[...]))
    for i, k, beam_ref in blocks:
        values = beam_ref[...].astype(F32)
        start = (me ^ k) * dishes
        for f in range(chans):
            for b in range(group_beams):
                for part in range(2):
                    first = (f * group_beams + b) * block + part * dishes
                    gathered[
                        (i * pairs + b * chans + f) * 2 + part,
                        pl.ds(start, dishes),
                        :,
                    ] = values[first : first + dishes]
    for pair in range(pairs):
        total = None
        for i in range(cycles):
            real = gathered[(i * pairs + pair) * 2]
            imag = gathered[(i * pairs + pair) * 2 + 1]
            top = jnp.concatenate([real, imag], axis=1)
            left = jnp.concatenate([top, jnp.concatenate([imag, -real], axis=1)]).astype(BF16)
            right = jnp.concatenate(
                [top, jnp.zeros((samples - pad_dishes, 2 * samples), F32)]
            ).astype(BF16)
            term = dot_t(left, right)
            total = term if total is None else total + term
        sums[pl.ds(pair, 2 * pad_dishes, stride=pad_pairs), :] = total * scale
    for part in range(2):
        pieces = []
        for d in range(all_dishes):
            first = (part * pad_dishes + d) * pad_pairs
            pieces.append(sums[first : first + pad_pairs, 0:all_dishes])
        flat = jnp.concatenate(pieces, axis=1)
        for b in range(group_beams):
            out_ref[part, b] = flat[b * chans : (b + 1) * chans]


def vmem():
    return pl.BlockSpec(memory_space=pltpu.VMEM)


def smem():
    return pl.BlockSpec(memory_space=pltpu.SMEM)


def per_device(voltages, weights, sat_index, offsets, angles):
    cycles, _, dishes, chans, ports, samples = voltages.shape
    beams = weights.shape[3]
    slots = sat_index.shape[2]
    groups = lax.axis_size("section")
    peers = lax.axis_size("chan")
    group_beams = beams // groups
    pad_beams = rounded_up(beams)
    assert cycles == 2 and chans == 2 and sat_index.shape[1] == 1
    assert groups > 1 and groups & (groups - 1) == 0
    dims = (groups, chans, group_beams, dishes, pad_beams)
    wide = ports * chans
    x = voltages.transpose(0, 1, 2, 4, 3, 5).reshape(cycles, 2, dishes, wide, samples)

    def swap(value, first):
        path = []
        for i in range(peers):
            other = i + 1 if i % 2 == first else i - 1
            for q in range(groups):
                to = other * groups + q if 0 <= other < peers else i * groups + (q ^ 1)
                path.append((i * groups + q, to))
        return lax.ppermute(value, ("chan", "section"), path)

    def params(**more):
        return pltpu.CompilerParams(vmem_limit_bytes=VMEM_GRANT, **more)

    def step_over(value, step):
        return lax.ppermute(value, "section", [(i, i ^ step) for i in range(groups)])

    sat_b = swap(sat_index, 1)
    sat_a = swap(sat_index, 0)

    chunk = 2 * chans * group_beams * dishes
    piece = jax.ShapeDtypeStruct((chunk, samples), BF16)
    two = jax.ShapeDtypeStruct((2, chunk, samples), BF16)
    several = jax.ShapeDtypeStruct((groups // 2 + 1, chunk, samples), BF16)
    stage = pltpu.VMEM((groups * stage_rows(dims), samples), F32)

    wide_rows = pl.pallas_call(
        functools.partial(spread_kernel, dims),
        out_shape=jax.ShapeDtypeStruct((dishes, 2, 2 * chans * pad_beams, wide), BF16),
        in_specs=[vmem()],
        out_specs=vmem(),
        compiler_params=params(),
        name="spread",
    )(weights)
    first_near, first_mine, *first_far = pl.pallas_call(
        functools.partial(first_beams_kernel, dims),
        out_shape=(piece, piece) + (two,) * (groups // 2 - 1),
        in_specs=[vmem()] * 2,
        out_specs=(vmem(),) * (groups // 2 + 1),
        scratch_shapes=[stage],
        compiler_params=params(),
        name="first_beams",
    )(x, wide_rows)
    first_got = [step_over(value, 2 * i + 2) for i, value in enumerate(first_far)]

    rows = chans * 2 * slots
    vectors = jax.ShapeDtypeStruct((dishes, 2 * slots, ports), F32)
    nulls = []
    for cycle in range(cycles):
        own, to_a, to_b = pl.pallas_call(
            functools.partial(nulls_kernel, cycle),
            out_shape=(vectors,) * 3,
            in_specs=[smem(), smem(), smem(), vmem(), vmem(), vmem()],
            out_specs=(vmem(),) * 3,
            scratch_shapes=[
                pltpu.VMEM((rows, ports), F32),
                pltpu.VMEM((dishes, 4 * rows, samples), F32),
                pltpu.VMEM((dishes * 2 * rows, wide), F32),
            ],
            compiler_params=params(),
        )(sat_index[:, 0], sat_a[:, 0], sat_b[:, 0], offsets, angles, x)
        from_b = swap(to_b, 1)
        from_a = swap(to_a, 0)
        nulls.append((own, from_a, from_b))

    next_rows = jax.ShapeDtypeStruct((dishes, 2 * chans * pad_beams, ports), BF16)
    second_near, second_mine, *second_far, w_next = pl.pallas_call(
        functools.partial(next_beams_kernel, dims, 0),
        out_shape=(several, piece) + (piece,) * (groups - 2) + (next_rows,),
        in_specs=[vmem()] * (5 + groups // 2),
        out_specs=(vmem(),) * (groups + 1),
        scratch_shapes=[stage],
        compiler_params=params(),
        name="next_beams",
    )(x, weights, *nulls[0], first_near, *first_got)
    second_got = [step_over(value, k + 2) for k, value in enumerate(second_far)]
    near_got = step_over(second_near, 1)

    new_weights = pl.pallas_call(
        functools.partial(last_nulls_kernel, dims),
        out_shape=jax.ShapeDtypeStruct(weights.shape, BF16),
        in_specs=[vmem()] * 4,
        out_specs=vmem(),
        compiler_params=params(),
        name="last_nulls",
    )(w_next, *nulls[1])

    all_dishes = dishes * groups
    pairs = group_beams * chans
    pad_dishes = rounded_up(all_dishes)
    vis = pl.pallas_call(
        functools.partial(correlate_kernel, dims, 1.0 / (cycles * samples)),
        out_shape=jax.ShapeDtypeStruct((2, group_beams, chans, all_dishes * all_dishes), F32),
        in_specs=[vmem()] * (3 + groups // 2 - 1 + groups - 2),
        out_specs=vmem(),
        scratch_shapes=[
            pltpu.VMEM((cycles * pairs * 2, pad_dishes, samples), F32),
            pltpu.VMEM((2 * pad_dishes * rounded_up(pairs), samples), F32),
        ],
        compiler_params=params(),
        name="correlate",
    )(first_mine, second_mine, near_got, *first_got, *second_got)
    return vis, new_weights


def solution(mesh):
    placed = (
        P(None, None, "section", "chan", None, None),
        P(None, "section", "chan", None, None),
        P(None, "chan", None),
        P(),
        P(),
    )
    return jax.shard_map(
        per_device,
        mesh=mesh,
        in_specs=placed,
        out_specs=(P(None, "section", "chan", None), P(None, "section", "chan", None, None)),
        check_vma=False,
    )
```
